256 devices in a mesh: gx: 64 (over z, y, core), gy: 4 (over x).
Axes of the slice: x: 4, y: 4, z: 8, core: 2. Of those that a mesh axis runs over, the one named last changes fastest.
Arguments:
- courant: float32 [512, 512, 256], P('gx', 'gy'), may hold values from 0.05 to 0.2
- first_moment: float32 [512, 512, 256], P('gx', 'gy'), may hold values from -6 to 6
- second_moment: float32 [512, 512, 256], P('gx', 'gy'), may hold values from 0.01 to 1
- adjoint_prev: float32 [512, 512, 256], P('gx', 'gy'), may hold values from -6 to 6
- adjoint_now: float32 [512, 512, 256], P('gx', 'gy'), may hold values from -6 to 6
- forward_field: bfloat16 [4, 512, 512, 256], P(None, 'gx', 'gy'), may hold values from -6 to 6
- traces: float32 [4, 8192, 128], P('gy', 'gx'), may hold values from -6 to 6
- trace_slab: int32 [4, 8192, 1], P('gy', 'gx'), may hold values from 0 to 63; in each aligned block of 128 rows (0 to 127, 128 to 255, ..., all dimensions but the last counted through in order) at most 4 rows name the same one
- trace_cell: int32 [4, 8192], P('gy', 'gx'), may hold values from 0 to 1023
- trace_shot: int32 [4, 8192], P('gy', 'gx'), may hold values from 0 to 15
- rollback: int32 [16], replicated, may hold values 0 or 1
Outputs:
- courant_next: float32 [512, 512, 256], P('gx', 'gy')
- first_next: float32 [512, 512, 256], P('gx', 'gy')
- second_next: float32 [512, 512, 256], P('gx', 'gy')
- adjoint_last: float32 [512, 512, 256], P('gx', 'gy')
The draws below stay inside these ranges and needn't reach their ends.
Inputs may be any that keep to these rules, and one draw needn't show every extreme that they name: `trace_slab`: within the 128 blocks of one device no x-slab is named by more than 4 blocks; in some devices one x-slab is named by exactly 4.
All inputs are finite; a program needn't handle non-finite values.
Results may differ from the reference program's by a relative error of at most 0.0003.
Values sent between devices are 32-bit elements; how exact they have to be, the bound alone decides.
A program may use at most 64 MiB of HBM per device.

```python
import math
import jax
import jax.numpy as jnp
import numpy as np
from jax import lax

CX = 8
CY = 128
NZ = 256
ADJOINT_STEPS = 4
SAMPLES = 128
SAMPLES_PER_STEP = 32
ZREC = 8
BLOCKS_PER_UNIT = 128
SHOTS = 16
CAP = 4
NX = 512
NY = 512
N_GX = 64
N_GY = 4


def set_ends(drawn, rng, low, largest):
    shape = drawn.shape
    spot = [jax.random.randint(jax.random.fold_in(rng, axis), (), 0, shape[axis]) for axis in range(len(shape))]
    drawn = drawn.at[tuple(spot)].set(low)
    longest = shape.index(max(shape))
    spot[longest] = (spot[longest] + 1) % shape[longest]
    return drawn.at[tuple(spot)].set(largest)


def level_of(key, extent, pieces, low, top_value):
    loudness = 1.0
    for dim, blocks in pieces:
        draws = jax.random.uniform(jax.random.fold_in(jax.random.fold_in(key, 6), dim), (blocks,), jnp.float32, low / len(pieces), top_value / len(pieces))
        loudness = loudness * jnp.repeat(jnp.exp(draws), extent[dim] // blocks).reshape((-1,) + (1,) * (len(extent) - 1 - dim))
    return loudness


def deal_out(own_key, own, number, rows, amount, top, most, skew):
    ranking = jax.random.permutation(own_key, amount)
    heavy_load, usual = shares(amount, rows * top, most, skew, True), shares(amount, rows * top, most, skew, False)
    places = jnp.arange(amount)

    def named(tallies, turn):
        used = int((tallies > 0).sum())
        fixed = max(1, used // 4)
        moved = fixed + (places - fixed + turn * (used - fixed)) % max(1, amount - fixed)
        return jnp.zeros((amount,), jnp.int32).at[ranking[jnp.where(places < fixed, places, moved)]].set(jnp.asarray(tallies, jnp.int32))

    tallies = jnp.where(number % 4 == 0, named(heavy_load, number // 4), named(usual, number - number // 4 - 1))
    mixed = jax.random.permutation(jax.random.fold_in(own, 3), amount)
    source_of, taker = mixed[0:amount // 2 * 2:2], mixed[1:amount // 2 * 2:2]
    slack = jnp.minimum(tallies[source_of] - 1, most - tallies[taker]) // 2
    slack = jnp.where((source_of == ranking[0]) | (taker == ranking[0]) | (tallies[taker] == 0), 0, jnp.maximum(slack, 0))
    moved = jax.random.randint(jax.random.fold_in(own, 4), (amount // 2,), 0, 1 << 20) % (slack + 1)
    tallies = tallies.at[source_of].add(-moved).at[taker].add(moved)
    labels = jnp.searchsorted(jnp.cumsum(tallies), jnp.arange(rows * top), side="right").astype(jnp.int32)
    listing = labels.reshape(top, rows).T
    listing = listing[jax.random.permutation(jax.random.fold_in(own, 1), rows)]
    turn = jax.random.randint(jax.random.fold_in(own, 2), (rows, 1), 0, top)
    return jnp.take_along_axis(listing, (jnp.arange(top)[None, :] + turn) % top, axis=1)


def shares(amount, total, most, skew, full):
    weights = [(1 << 20) // math.isqrt(rank ** skew) + 1 for rank in range(1, amount + 1)]
    largest = most if full else min(most, max(-(-total // amount), total * weights[0] // sum(weights)))
    least = 1 if total - largest >= amount - 1 else 0
    holding, spare = [largest] + [least] * (amount - 1), total - largest - least * (amount - 1)
    while spare > 0:
        candidates = [i for i in range(1, amount) if holding[i] < largest] or [i for i in range(1, amount) if holding[i] < most]
        whole, remaining = sum([weights[i] for i in candidates]), spare
        for i in candidates:
            extra = min(most - holding[i], max(1, remaining * weights[i] // whole), spare)
            holding[i] = holding[i] + extra
            spare = spare - extra
    return np.array(holding)


def bell_draw(key, dims, width, reach, split=(), kind=jnp.bfloat16):
    values = width * jax.random.normal(key, dims, jnp.float32)
    if split:
        values = values * level_of(key, dims, split, -0.22, 0.18)
    return jnp.clip(values, -reach, reach).astype(kind)


def setup_inputs(seed: int = 0) -> dict:
    key_of = jax.random.split(jax.random.key(seed), 12)
    courant = jnp.clip(jnp.exp(math.log(0.2) - 1.3862944 * jax.random.uniform(key_of[0], (NX, NY, NZ), jnp.float32) ** level_of(key_of[0], (NX, NY, NZ), ((0, 64), (1, 4)), -0.2, 0.2)), 0.05, 0.2)
    first_moment = bell_draw(key_of[1], (NX, NY, NZ), 1.0, 6.0, ((0, 64), (1, 4)), jnp.float32)
    second_moment = jnp.clip(jnp.exp(math.log(1.0) - 4.6051702 * jax.random.uniform(key_of[2], (NX, NY, NZ), jnp.float32) ** level_of(key_of[2], (NX, NY, NZ), ((0, 64), (1, 4)), -0.2, 0.2)), 0.01, 1.0)
    adjoint_prev = bell_draw(key_of[3], (NX, NY, NZ), 1.0, 6.0, ((0, 64), (1, 4)), jnp.float32)
    adjoint_now = bell_draw(key_of[4], (NX, NY, NZ), 1.0, 6.0, ((0, 64), (1, 4)), jnp.float32)
    forward_field = bell_draw(key_of[5], (ADJOINT_STEPS, NX, NY, NZ), 1.0, 6.0, ((1, 64), (2, 4)))
    traces = bell_draw(key_of[6], (N_GY, N_GX * BLOCKS_PER_UNIT, SAMPLES), 1.0, 6.0, ((0, 4), (1, 64)), jnp.float32)
    trace_slab_keys = jax.random.split(jax.random.fold_in(key_of[7], 1), N_GY * (N_GX * BLOCKS_PER_UNIT) // BLOCKS_PER_UNIT)
    trace_slab_turns = jax.random.permutation(jax.random.fold_in(key_of[7], 3), N_GY * (N_GX * BLOCKS_PER_UNIT) // BLOCKS_PER_UNIT)
    trace_slab = jax.vmap(lambda own, number: deal_out(jax.random.fold_in(key_of[7], 2), own, number, BLOCKS_PER_UNIT, N_GX, 1, CAP, 2))(trace_slab_keys, trace_slab_turns).reshape((N_GY, N_GX * BLOCKS_PER_UNIT, 1))
    trace_cell = set_ends(jax.random.randint(key_of[8], (N_GY, N_GX * BLOCKS_PER_UNIT), 0, CX * CY), jax.random.fold_in(key_of[8], 1), 0, (CX * CY) - 1).astype(jnp.int32)
    trace_shot = set_ends(jax.random.randint(key_of[9], (N_GY, N_GX * BLOCKS_PER_UNIT), 0, SHOTS), jax.random.fold_in(key_of[9], 1), 0, SHOTS - 1).astype(jnp.int32)
    rollback = set_ends((jax.random.randint(key_of[10], (SHOTS,), 0, 4) < 1).astype(jnp.int32), jax.random.fold_in(key_of[10], 1), 0, 1)
    return dict(courant=courant, first_moment=first_moment, second_moment=second_moment, adjoint_prev=adjoint_prev, adjoint_now=adjoint_now, forward_field=forward_field, traces=traces, trace_slab=trace_slab, trace_cell=trace_cell, trace_shot=trace_shot, rollback=rollback)


coefficients = (8.0 / 5.0, -1.0 / 5.0, 8.0 / 315.0, -1.0 / 560.0)
center_weight = -205.0 / 72.0
smooth_length = 4096.0
cosh_value = 1.0 + 0.5 / smooth_length
theta = math.log(cosh_value + math.sqrt(cosh_value * cosh_value - 1.0))
image_gain = 10.0
beta_first = 0.9
beta_second = 0.999
bias_first = 1.0 - 0.9 ** 10
bias_second = 1.0 - 0.999 ** 10
learning_rate = 0.01
epsilon = 1e-08

def smoother(count):
    position = jnp.arange(count, dtype=jnp.int32).astype(jnp.float32)
    lower = jnp.minimum(position[:, None], position[None, :])
    upper = jnp.maximum(position[:, None], position[None, :])
    spread = jnp.abs(position[:, None] - position[None, :])
    numerator = jnp.exp(-theta * spread) * (1.0 - jnp.exp(-2.0 * theta * (lower + 1.0))) * (1.0 - jnp.exp(-2.0 * theta * (count - upper)))
    denominator = 2.0 * smooth_length * math.sinh(theta) * (1.0 - math.exp(-2.0 * theta * (count + 1)))
    return numerator / denominator

def stencil_sum(padded, wavefield):
    length_x, length_y, length_z = wavefield.shape
    summed = 3.0 * center_weight * wavefield
    for offset, weight in enumerate(coefficients, 1):
        paired = padded[4 + offset:4 + offset + length_x, 4:4 + length_y, 4:4 + length_z]
        paired = paired + padded[4 - offset:4 - offset + length_x, 4:4 + length_y, 4:4 + length_z]
        paired = paired + padded[4:4 + length_x, 4 + offset:4 + offset + length_y, 4:4 + length_z]
        paired = paired + padded[4:4 + length_x, 4 - offset:4 - offset + length_y, 4:4 + length_z]
        paired = paired + padded[4:4 + length_x, 4:4 + length_y, 4 + offset:4 + offset + length_z]
        paired = paired + padded[4:4 + length_x, 4:4 + length_y, 4 - offset:4 - offset + length_z]
        summed = summed + weight * paired
    return summed

def reference(courant, first_moment, second_moment, adjoint_prev, adjoint_now, forward_field, traces, trace_slab, trace_cell, trace_shot, rollback):
    active_mask = (rollback[trace_shot] == 0).astype(jnp.float32)
    thinned_traces = traces.reshape(N_GY, N_GX * BLOCKS_PER_UNIT, ADJOINT_STEPS, SAMPLES_PER_STEP).sum(axis=-1) * active_mask[..., None]
    x_cells = trace_slab[..., 0] * CX + trace_cell // CY
    y_cells = jnp.arange(N_GY, dtype=jnp.int32)[:, None] * CY + trace_cell % CY
    source = jnp.zeros((ADJOINT_STEPS, NX, NY), jnp.float32).at[:, x_cells.reshape(-1), y_cells.reshape(-1)].add(thinned_traces.reshape(-1, ADJOINT_STEPS).T)
    previous = adjoint_prev
    current = adjoint_now
    image = jnp.zeros(courant.shape, jnp.float32)
    for step_index in range(ADJOINT_STEPS):
        padded = jnp.pad(current, 4)
        following = 2.0 * current - previous + courant * stencil_sum(padded, current)
        following = following.at[:, :, ZREC].add(source[step_index])
        image = image + forward_field[step_index].astype(jnp.float32) * following
        previous, current = (current, following)
    gradient = image_gain * image
    table = smoother(NX)
    smoothed = jnp.dot(table, gradient.reshape(NX, -1), precision=lax.Precision.HIGHEST, preferred_element_type=jnp.float32).reshape(NX, NY, NZ)
    first_next = beta_first * first_moment + (1.0 - beta_first) * smoothed
    second_next = beta_second * second_moment + (1.0 - beta_second) * smoothed * smoothed
    courant_next = courant - learning_rate * (first_next / bias_first) / (jnp.sqrt(second_next / bias_second) + epsilon)
    return (courant_next, first_next, second_next, current)
```

```python
import math

import jax
import jax.numpy as jnp
import numpy as np
from jax import lax
from jax.experimental import pallas as pl
from jax.experimental.pallas import tpu as pltpu
from jax.sharding import PartitionSpec as P

MESH = pl.DeviceIdType.MESH
F32 = jnp.float32
HIGHEST = lax.Precision.HIGHEST

STEPS = 4
SAMPLES_PER_STEP = 32
ZREC = 8
SHOTS = 16
NG = 64
NYD = 4
NQ = 8
NZD = 8
CX, CY, NZ = 8, 128, 256
BLOCKS = 128
SLOTS = 4
ROWS = 32
CHUNKS = CY // ROWS
SEG = CY // NQ

coefficients = (8.0 / 5.0, -1.0 / 5.0, 8.0 / 315.0, -1.0 / 560.0)
center_weight = -205.0 / 72.0
smooth_length = 4096.0
cosh_value = 1.0 + 0.5 / smooth_length
theta = math.log(cosh_value + math.sqrt(cosh_value * cosh_value - 1.0))
image_gain = 10.0
beta_first = 0.9
beta_second = 0.999
bias_first = 1.0 - 0.9**10
bias_second = 1.0 - 0.999**10
learning_rate = 0.01
epsilon = 1e-08


def depth_table():
    table = np.zeros((NZ, NZ), np.float64)
    for i in range(NZ):
        table[i, i] = 3.0 * center_weight
        for k, w in enumerate(coefficients, 1):
            if i + k < NZ:
                table[i + k, i] = w
                table[i, i + k] = w
    return table.astype(np.float32)


def smoother_factors(count):
    position = np.arange(count, dtype=np.float64)
    scale = math.sqrt(image_gain / (smooth_length * math.sinh(theta) * math.sinh(theta * (count + 1))))
    rise = scale * np.sinh(theta * (position + 1.0))
    fall = scale * np.sinh(theta * (count - position))
    return np.concatenate([rise, fall]).astype(np.float32)


def iota(shape, dim):
    return lax.broadcasted_iota(jnp.int32, shape, dim)


def window_kernel(
    rollback_ref,
    factor_ref,
    table_ref,
    traces_ref,
    slab_ref,
    cell_ref,
    shot_ref,
    courant_hbm,
    prev_hbm,
    now_hbm,
    forward_hbm,
    image_hbm,
    last_hbm,
    sums_hbm,
    field,
    courant,
    forward,
    image,
    source,
    packed,
    landed,
    depth,
    plane,
    group_in,
    total,
    line_in,
    back,
    sums,
    load_sem,
    trace_send,
    trace_recv,
    x_send,
    x_recv,
    y_send,
    y_recv,
    group_send,
    group_recv,
    line_send,
    line_recv,
    back_send,
    back_recv,
    store_sem,
):
    gx = lax.axis_index("gx")
    gy = lax.axis_index("gy")
    own_z = gx // NQ
    own_q = gx % NQ

    loads = [
        pltpu.make_async_copy(
            now_hbm, field.at[0, pl.ds(4, CX), pl.ds(8, CY), :], load_sem.at[0]
        ),
        pltpu.make_async_copy(
            prev_hbm, field.at[1, pl.ds(4, CX), pl.ds(8, CY), :], load_sem.at[1]
        ),
        pltpu.make_async_copy(courant_hbm, courant, load_sem.at[2]),
        pltpu.make_async_copy(forward_hbm, forward, load_sem.at[3]),
    ]
    for copy in loads:
        copy.start()

    @pl.when(gx == 0)
    def _():
        field[:, 0:4, 8 : 8 + CY, :] = jnp.zeros((2, 4, CY, NZ), F32)

    @pl.when(gx == NG - 1)
    def _():
        field[:, 12:16, 8 : 8 + CY, :] = jnp.zeros((2, 4, CY, NZ), F32)

    @pl.when(gy == 0)
    def _():
        field[:, 4:12, 0:8, :] = jnp.zeros((2, CX, 8, NZ), F32)

    @pl.when(gy == NYD - 1)
    def _():
        field[:, 4:12, 8 + CY : 16 + CY, :] = jnp.zeros((2, CX, 8, NZ), F32)

    barrier = pltpu.get_barrier_semaphore()

    def greet(k, carry):
        pl.semaphore_signal(
            barrier, inc=1, device_id={"gx": (gx + k) % NG}, device_id_type=MESH
        )
        return carry

    lax.fori_loop(1, NG, greet, 0)
    for k in (1, NYD - 1):
        pl.semaphore_signal(
            barrier, inc=1, device_id={"gy": (gy + k) % NYD}, device_id_type=MESH
        )

    rows = iota((BLOCKS, 128), 0)
    lanes = iota((BLOCKS, 128), 1)
    diagonal = rows == lanes
    slab_col = slab_ref[0]
    shot_row = shot_ref[...]
    cell_row = cell_ref[...].astype(F32)
    live_row = jnp.zeros((1, 128), F32)
    for s in range(SHOTS):
        flag = jnp.where(rollback_ref[s] == 0, 1.0, 0.0)
        live_row = jnp.where(shot_row == s, flag, live_row)
    live_col = jnp.sum(jnp.where(diagonal, live_row, 0.0), axis=1, keepdims=True)
    cell_col = jnp.sum(jnp.where(diagonal, cell_row, 0.0), axis=1, keepdims=True)
    slab_float = slab_col.astype(F32)
    slab_row = jnp.sum(jnp.where(diagonal, slab_float, 0.0), axis=0, keepdims=True)
    slot_col = jnp.sum(
        jnp.where((slab_float == slab_row) & (lanes < rows), 1.0, 0.0), axis=1, keepdims=True
    )
    pick = jnp.where((lanes % 8 == rows // SAMPLES_PER_STEP) & (lanes < 8 * SLOTS), 1.0, 0.0)
    reduced = jnp.dot(traces_ref[0], pick, precision=HIGHEST, preferred_element_type=F32)
    entries = reduced * live_col + jnp.where(lanes % 8 == STEPS, cell_col, 0.0)
    entries = jnp.where(slot_col == (lanes // 8).astype(F32), entries, 0.0)
    named = jnp.where(iota((NG, BLOCKS), 0).astype(F32) == slab_row, 1.0, 0.0)
    packed[...] = jnp.dot(
        named, entries, precision=HIGHEST, preferred_element_type=F32
    ).reshape(NG, 1, 128)

    pl.semaphore_wait(barrier, NG - 1 + 2)

    def x_copies(parity, chunk, source_low, source_high):
        band = pl.ds(pl.multiple_of(8 + chunk * ROWS, 8), ROWS)
        low = pltpu.make_async_remote_copy(
            src_ref=source_low,
            dst_ref=field.at[parity, pl.ds(12, 4), band, :],
            send_sem=x_send.at[parity, 0, chunk],
            recv_sem=x_recv.at[parity, 1, chunk],
            device_id={"gx": (gx + NG - 1) % NG},
            device_id_type=MESH,
        )
        high = pltpu.make_async_remote_copy(
            src_ref=source_high,
            dst_ref=field.at[parity, pl.ds(0, 4), band, :],
            send_sem=x_send.at[parity, 1, chunk],
            recv_sem=x_recv.at[parity, 0, chunk],
            device_id={"gx": (gx + 1) % NG},
            device_id_type=MESH,
        )
        return low, high

    def x_field(parity, chunk):
        band = pl.ds(pl.multiple_of(8 + chunk * ROWS, 8), ROWS)
        return x_copies(
            parity, chunk, field.at[parity, pl.ds(4, 4), band, :], field.at[parity, pl.ds(8, 4), band, :]
        )

    def y_copies(parity, source_low, source_high):
        low = pltpu.make_async_remote_copy(
            src_ref=source_low,
            dst_ref=field.at[parity, pl.ds(4, CX), pl.ds(8 + CY, 8), :],
            send_sem=y_send.at[parity, 0],
            recv_sem=y_recv.at[parity, 1],
            device_id={"gy": (gy + NYD - 1) % NYD},
            device_id_type=MESH,
        )
        high = pltpu.make_async_remote_copy(
            src_ref=source_high,
            dst_ref=field.at[parity, pl.ds(4, CX), pl.ds(0, 8), :],
            send_sem=y_send.at[parity, 1],
            recv_sem=y_recv.at[parity, 0],
            device_id={"gy": (gy + 1) % NYD},
            device_id_type=MESH,
        )
        return low, high

    def y_field(parity):
        return y_copies(
            parity,
            field.at[parity, pl.ds(4, CX), pl.ds(8, 8), :],
            field.at[parity, pl.ds(4, CX), pl.ds(CY, 8), :],
        )

    has_low, has_high = gx > 0, gx < NG - 1
    y_has_low, y_has_high = gy > 0, gy < NYD - 1

    def order(i):
        return (CHUNKS - i) % CHUNKS

    now_low, now_high = y_copies(0, now_hbm.at[:, pl.ds(0, 8), :], now_hbm.at[:, pl.ds(CY - 8, 8), :])
    pl.when(y_has_low)(now_low.start)
    pl.when(y_has_high)(now_high.start)

    def send_now(i, carry):
        chunk = order(i)
        band = pl.ds(pl.multiple_of(chunk * ROWS, 8), ROWS)
        low, high = x_copies(
            0, chunk, now_hbm.at[pl.ds(0, 4), band, :], now_hbm.at[pl.ds(4, 4), band, :]
        )
        pl.when(has_low)(low.start)
        pl.when(has_high)(high.start)
        return carry

    def trace_copy(peer, mine):
        return pltpu.make_async_remote_copy(
            src_ref=packed.at[peer],
            dst_ref=landed.at[mine],
            send_sem=trace_send.at[peer],
            recv_sem=trace_recv.at[mine],
            device_id={"gx": peer},
            device_id_type=MESH,
        )

    def send_traces(k, carry):
        trace_copy((gx + k) % NG, gx).start()
        return carry

    lax.fori_loop(1, NG, send_traces, 0)
    lax.fori_loop(0, CHUNKS, send_now, 0)

    landed[gx] = packed[gx]

    def wait_traces(k, carry):
        peer = (gx + k) % NG
        trace_copy(peer, peer).wait_recv()
        return carry

    lax.fori_loop(1, NG, wait_traces, 0)

    def wait_trace_sends(k, carry):
        peer = (gx + k) % NG
        trace_copy(peer, peer).wait_send()
        return carry

    lax.fori_loop(1, NG, wait_trace_sends, 0)

    arrived = landed[...].reshape(NG, 128)
    lane = iota((NG, 128), 1)
    spread = jnp.zeros((CY, 128), F32)
    for j in range(SLOTS):
        cell = arrived[:, 8 * j + STEPS : 8 * j + STEPS + 1].astype(jnp.int32)
        weights = jnp.zeros((NG, 128), F32)
        for t in range(STEPS):
            weights = jnp.where(lane // CX == t, arrived[:, 8 * j + t : 8 * j + t + 1], weights)
        weights = jnp.where(lane % CX == cell // CY, weights, 0.0)
        spot = jnp.where(lane == cell % CY, 1.0, 0.0)
        spread = spread + lax.dot_general(
            spot, weights, (((0,), (0,)), ((), ())), precision=HIGHEST, preferred_element_type=F32
        )
    at_depth = iota((CY, 128), 1) == ZREC
    for c in range(STEPS * CX):
        source[c] = jnp.where(at_depth, spread[:, c : c + 1], 0.0)

    for copy in loads:
        copy.wait()

    eight = iota((8, NZ), 0)

    def advance(t):
        now, later = t % 2, (t + 1) % 2

        def chunk_body(i, carry):
            chunk = order(i)
            low, high = x_field(now, chunk)
            pl.when(has_low)(high.wait_recv)
            pl.when(has_high)(low.wait_recv)
            if t >= 1:
                old_low, old_high = x_field(later, chunk)
                pl.when(has_low)(old_low.wait_send)
                pl.when(has_high)(old_high.wait_send)

            @pl.when(i == 0)
            def _():
                y_low, y_high = y_field(now)
                pl.when(y_has_low)(y_high.wait_recv)
                pl.when(y_has_high)(y_low.wait_recv)
                if t >= 1:
                    y_old_low, y_old_high = y_field(later)
                    pl.when(y_has_low)(y_old_low.wait_send)
                    pl.when(y_has_high)(y_old_high.wait_send)

            base = pl.multiple_of(chunk * ROWS, ROWS)
            depth[...] = jnp.dot(
                field[now, 4:12, pl.ds(base + 8, ROWS), :].reshape(CX * ROWS, NZ),
                table_ref[...],
                precision=HIGHEST,
                preferred_element_type=F32,
            ).reshape(CX, ROWS, NZ)

            def row_body(j, carry):
                top = pl.multiple_of(base + j * 16, 16)
                for x in range(CX):
                    wave = forward[t, x, pl.ds(top, 16), :].astype(F32)
                    for half in range(2):
                        inner = pl.multiple_of(j * 16 + half * 8, 8)
                        row = pl.multiple_of(top + half * 8, 8)
                        r = pl.ds(pl.multiple_of(row + 8, 8), 8)
                        mid = field[now, 4 + x, r, :]
                        above = field[now, 4 + x, pl.ds(row, 8), :]
                        below = field[now, 4 + x, pl.ds(pl.multiple_of(row + 16, 8), 8), :]
                        total_sum = depth[x, pl.ds(inner, 8), :]
                        for k, w in enumerate(coefficients, 1):
                            paired = field[now, 4 + x + k, r, :] + field[now, 4 + x - k, r, :]
                            paired += pltpu.roll(jnp.where(eight >= k, mid, below), 8 - k, 0)
                            paired += pltpu.roll(jnp.where(eight < 8 - k, mid, above), k, 0)
                            total_sum += w * paired
                        out_rows = pl.ds(row, 8)
                        following = (
                            2.0 * mid
                            - field[later, 4 + x, r, :]
                            + courant[x, out_rows, :] * total_sum
                        )
                        following = jnp.concatenate(
                            [
                                following[:, :128] + source[t * CX + x, out_rows, :],
                                following[:, 128:],
                            ],
                            axis=1,
                        )
                        field[later, 4 + x, r, :] = following
                        term = wave[half * 8 : half * 8 + 8] * following
                        if t == 0:
                            image[x, out_rows, :] = term
                        else:
                            image[x, out_rows, :] += term
                return carry

            lax.fori_loop(0, ROWS // 16, row_body, 0)

            if t < STEPS - 1:
                next_low, next_high = x_field(later, chunk)
                pl.when(has_low)(next_low.start)
                pl.when(has_high)(next_high.start)

                y_low, y_high = y_field(later)

                @pl.when(i == 0)
                def _():
                    pl.when(y_has_low)(y_low.start)

                @pl.when(i == 1)
                def _():
                    pl.when(y_has_high)(y_high.start)

            return carry

        lax.fori_loop(0, CHUNKS, chunk_body, 0)

    for t in range(STEPS):
        advance(t)

    store_last = pltpu.make_async_copy(
        field.at[STEPS % 2, pl.ds(4, CX), pl.ds(8, CY), :], last_hbm, store_sem.at[0]
    )
    store_image = pltpu.make_async_copy(image, image_hbm, store_sem.at[1])
    store_last.start()
    store_image.start()

    def weigh(j, carry):
        r = pl.ds(pl.multiple_of(j * 8, 8), 8)
        up = jnp.zeros((8, NZ), F32)
        down = jnp.zeros((8, NZ), F32)
        for x in range(CX):
            value = image[x, r, :]
            up += factor_ref[gx * CX + x] * value
            down += factor_ref[NG * CX + gx * CX + x] * value
        plane[0, r, :] = up
        plane[1, r, :] = down
        return carry

    lax.fori_loop(0, CY // 8, weigh, 0)

    def segment(q):
        return pl.ds(pl.multiple_of(q * SEG, SEG), SEG)

    def group_copy(peer, mine):
        return pltpu.make_async_remote_copy(
            src_ref=plane.at[:, segment(peer), :],
            dst_ref=group_in.at[mine],
            send_sem=group_send.at[peer],
            recv_sem=group_recv.at[mine],
            device_id={"gx": own_z * NQ + peer},
            device_id_type=MESH,
        )

    def line_copy(k):
        peer = (own_z + k) % NZD
        return pltpu.make_async_remote_copy(
            src_ref=total.at[(own_z + k) // NZD],
            dst_ref=line_in.at[own_z],
            send_sem=line_send.at[peer],
            recv_sem=line_recv.at[own_z],
            device_id={"gx": peer * NQ + own_q},
            device_id_type=MESH,
        )

    def line_arrival(k):
        peer = (own_z + k) % NZD
        return pltpu.make_async_remote_copy(
            src_ref=total.at[0],
            dst_ref=line_in.at[peer],
            send_sem=line_send.at[peer],
            recv_sem=line_recv.at[peer],
            device_id={"gx": peer * NQ + own_q},
            device_id_type=MESH,
        )

    def back_copy(peer, mine):
        return pltpu.make_async_remote_copy(
            src_ref=back.at[peer],
            dst_ref=sums.at[:, segment(mine), :],
            send_sem=back_send.at[peer],
            recv_sem=back_recv.at[mine],
            device_id={"gx": own_z * NQ + peer},
            device_id_type=MESH,
        )

    for k in range(1, NQ):
        group_copy((own_q + k) % NQ, own_q).start()
    group_in[own_q] = plane[:, segment(own_q), :]
    for k in range(1, NQ):
        peer = (own_q + k) % NQ
        group_copy(peer, peer).wait_recv()

    below_sum = group_in[0, 0]
    above_sum = group_in[NQ - 1, 1]
    for q in range(1, NQ):
        below_sum = below_sum + group_in[q, 0]
        above_sum = above_sum + group_in[NQ - 1 - q, 1]
    total[0] = below_sum
    total[1] = above_sum

    for k in range(1, NZD):
        line_copy(k).start()
    line_in[own_z] = jnp.zeros((SEG, NZ), F32)
    for k in range(1, NZD):
        line_arrival(k).wait_recv()

    low_sum = jnp.zeros((SEG, NZ), F32)
    high_sum = jnp.zeros((SEG, NZ), F32)
    for z in range(NZD):
        part = line_in[z]
        low_sum = low_sum + jnp.where(z < own_z, part, 0.0)
        high_sum = high_sum + jnp.where(z > own_z, part, 0.0)
    for q in range(NQ):
        back[q, 0] = low_sum
        low_sum = low_sum + group_in[q, 0]
        back[NQ - 1 - q, 1] = high_sum
        high_sum = high_sum + group_in[NQ - 1 - q, 1]

    for k in range(1, NQ):
        back_copy((own_q + k) % NQ, own_q).start()
    sums[:, segment(own_q), :] = back[own_q]
    for k in range(1, NQ):
        peer = (own_q + k) % NQ
        back_copy(peer, peer).wait_recv()

    store_sums = pltpu.make_async_copy(sums, sums_hbm, store_sem.at[2])
    store_sums.start()

    for k in range(1, NQ):
        peer = (own_q + k) % NQ
        group_copy(peer, peer).wait_send()
        back_copy(peer, peer).wait_send()
    for k in range(1, NZD):
        line_arrival(k).wait_send()
    def wait_sends(i, carry):
        low, high = x_field((STEPS - 1) % 2, i)
        pl.when(has_low)(low.wait_send)
        pl.when(has_high)(high.wait_send)
        return carry

    lax.fori_loop(0, CHUNKS, wait_sends, 0)
    low, high = y_field((STEPS - 1) % 2)
    pl.when(y_has_low)(low.wait_send)
    pl.when(y_has_high)(high.wait_send)
    store_last.wait()
    store_image.wait()
    store_sums.wait()


def update_kernel(
    factor_ref,
    image_ref,
    sums_ref,
    last_ref,
    courant_ref,
    first_ref,
    second_ref,
    courant_out,
    first_out,
    second_out,
    last_out,
):
    gx = lax.axis_index("gx")
    last_out[...] = last_ref[...]
    rows = image_ref.shape[1]

    def body(j, carry):
        r = pl.ds(pl.multiple_of(j * 8, 8), 8)
        low = sums_ref[0, r, :]
        high = sums_ref[1, r, :]
        values = [image_ref[x, r, :] for x in range(CX)]
        rise = [factor_ref[gx * CX + x] for x in range(CX)]
        fall = [factor_ref[NG * CX + gx * CX + x] for x in range(CX)]
        below = []
        for x in range(CX):
            low = low + rise[x] * values[x]
            below.append(low)
        for x in reversed(range(CX)):
            smoothed = fall[x] * below[x] + rise[x] * high
            high = high + fall[x] * values[x]
            first = beta_first * first_ref[x, r, :] + (1.0 - beta_first) * smoothed
            second = beta_second * second_ref[x, r, :] + (1.0 - beta_second) * smoothed * smoothed
            first_out[x, r, :] = first
            second_out[x, r, :] = second
            courant_out[x, r, :] = courant_ref[x, r, :] - learning_rate * (first / bias_first) / (
                jnp.sqrt(second / bias_second) + epsilon
            )
        return carry

    lax.fori_loop(0, rows // 8, body, 0)


def shards(
    courant,
    first_moment,
    second_moment,
    adjoint_prev,
    adjoint_now,
    forward_field,
    traces,
    trace_slab,
    trace_cell,
    trace_shot,
    rollback,
):
    factors = jnp.asarray(smoother_factors(NG * CX))
    table = jnp.asarray(depth_table())
    shape = jax.ShapeDtypeStruct((CX, CY, NZ), F32)
    anywhere = pl.BlockSpec(memory_space=pl.ANY)
    smem = pl.BlockSpec(memory_space=pltpu.SMEM)
    vmem = pl.BlockSpec(memory_space=pltpu.VMEM)
    dma = pltpu.SemaphoreType.DMA
    image, last, sums = pl.pallas_call(
        window_kernel,
        out_shape=(shape, shape, jax.ShapeDtypeStruct((2, CY, NZ), F32)),
        in_specs=[smem, smem, vmem, vmem, vmem, vmem, vmem] + [anywhere] * 4,
        out_specs=(anywhere,) * 3,
        scratch_shapes=[
            pltpu.VMEM((2, CX + 8, CY + 16, NZ), F32),
            pltpu.VMEM((CX, CY, NZ), F32),
            pltpu.VMEM((STEPS, CX, CY, NZ), jnp.bfloat16),
            pltpu.VMEM((CX, CY, NZ), F32),
            pltpu.VMEM((STEPS * CX, CY, 128), F32),
            pltpu.VMEM((NG, 1, 128), F32),
            pltpu.VMEM((NG, 1, 128), F32),
            pltpu.VMEM((CX, ROWS, NZ), F32),
            pltpu.VMEM((2, CY, NZ), F32),
            pltpu.VMEM((NQ, 2, SEG, NZ), F32),
            pltpu.VMEM((2, SEG, NZ), F32),
            pltpu.VMEM((NZD, SEG, NZ), F32),
            pltpu.VMEM((NQ, 2, SEG, NZ), F32),
            pltpu.VMEM((2, CY, NZ), F32),
            dma((4,)),
            dma((NG,)),
            dma((NG,)),
            dma((2, 2, CHUNKS)),
            dma((2, 2, CHUNKS)),
            dma((2, 2)),
            dma((2, 2)),
            dma((NQ,)),
            dma((NQ,)),
            dma((NZD,)),
            dma((NZD,)),
            dma((NQ,)),
            dma((NQ,)),
            dma((3,)),
        ],
        compiler_params=pltpu.CompilerParams(
            collective_id=0, has_side_effects=True, vmem_limit_bytes=24 << 20
        ),
    )(
        rollback,
        factors,
        table,
        traces,
        trace_slab,
        trace_cell,
        trace_shot,
        courant,
        adjoint_prev,
        adjoint_now,
        forward_field,
    )

    tile = 32
    block = pl.BlockSpec((CX, tile, NZ), lambda i: (0, i, 0))
    plane = pl.BlockSpec((2, tile, NZ), lambda i: (0, i, 0))
    return pl.pallas_call(
        update_kernel,
        grid=(CY // tile,),
        out_shape=(shape,) * 4,
        in_specs=[smem, block, plane, block, block, block, block],
        out_specs=(block,) * 4,
        compiler_params=pltpu.CompilerParams(vmem_limit_bytes=24 << 20),
    )(factors, image, sums, last, courant, first_moment, second_moment)


def solution(mesh):
    in_specs = (
        P("gx", "gy", None),
        P("gx", "gy", None),
        P("gx", "gy", None),
        P("gx", "gy", None),
        P("gx", "gy", None),
        P(None, "gx", "gy", None),
        P("gy", "gx", None),
        P("gy", "gx", None),
        P("gy", "gx"),
        P("gy", "gx"),
        P(),
    )
    out_specs = (P("gx", "gy", None),) * 4
    return jax.shard_map(shards, mesh=mesh, in_specs=in_specs, out_specs=out_specs, check_vma=False)
```

```python
import math

import jax
import jax.numpy as jnp
import numpy as np
from jax import lax
from jax.experimental import pallas as pl
from jax.experimental.pallas import tpu as pltpu
from jax.sharding import PartitionSpec as P

MESH = pl.DeviceIdType.MESH
F32 = jnp.float32
HIGHEST = lax.Precision.HIGHEST

STEPS = 4
SAMPLES_PER_STEP = 32
ZREC = 8
SHOTS = 16
NG = 64
NYD = 4
NQ = 8
NZD = 8
CX, CY, NZ = 8, 128, 256
BLOCKS = 128
SLOTS = 4
ROWS = 32
CHUNKS = CY // ROWS
UPDATE_ROWS = 32
SEG = CY // NQ

coefficients = (8.0 / 5.0, -1.0 / 5.0, 8.0 / 315.0, -1.0 / 560.0)
center_weight = -205.0 / 72.0
smooth_length = 4096.0
cosh_value = 1.0 + 0.5 / smooth_length
theta = math.log(cosh_value + math.sqrt(cosh_value * cosh_value - 1.0))
image_gain = 10.0
beta_first = 0.9
beta_second = 0.999
bias_first = 1.0 - 0.9**10
bias_second = 1.0 - 0.999**10
learning_rate = 0.01
epsilon = 1e-08


def depth_table():
    table = np.zeros((NZ, NZ), np.float64)
    for i in range(NZ):
        table[i, i] = 3.0 * center_weight
        for k, w in enumerate(coefficients, 1):
            if i + k < NZ:
                table[i + k, i] = w
                table[i, i + k] = w
    return table.astype(np.float32)


def smoother_factors(count):
    position = np.arange(count, dtype=np.float64)
    scale = math.sqrt(image_gain / (smooth_length * math.sinh(theta) * math.sinh(theta * (count + 1))))
    rise = scale * np.sinh(theta * (position + 1.0))
    fall = scale * np.sinh(theta * (count - position))
    return np.concatenate([rise, fall]).astype(np.float32)


def iota(shape, dim):
    return lax.broadcasted_iota(jnp.int32, shape, dim)


def window_kernel(
    rollback_hbm,
    factor_hbm,
    table_hbm,
    traces_hbm,
    slab_hbm,
    cell_hbm,
    shot_hbm,
    courant_hbm,
    prev_hbm,
    now_hbm,
    forward_hbm,
    image_hbm,
    last_hbm,
    sums_hbm,
    rollback_ref,
    factor_ref,
    table_ref,
    traces_ref,
    slab_ref,
    cell_ref,
    shot_ref,
    field,
    courant,
    forward,
    image,
    source,
    packed,
    landed,
    depth,
    plane,
    group_in,
    total,
    line_in,
    back,
    sums,
    load_sem,
    trace_send,
    trace_recv,
    x_send,
    x_recv,
    y_send,
    y_recv,
    group_send,
    group_recv,
    line_send,
    line_recv,
    back_send,
    back_recv,
    store_sem,
):
    gx = lax.axis_index("gx")
    gy = lax.axis_index("gy")
    own_z = gx // NQ
    own_q = gx % NQ

    small = [
        pltpu.make_async_copy(source_ref, target_ref, load_sem.at[4 + k])
        for k, (source_ref, target_ref) in enumerate(
            (
                (traces_hbm, traces_ref),
                (slab_hbm, slab_ref),
                (cell_hbm, cell_ref),
                (shot_hbm, shot_ref),
                (rollback_hbm, rollback_ref),
                (table_hbm, table_ref),
                (factor_hbm, factor_ref),
            )
        )
    ]
    for copy in small:
        copy.start()
    loads = [
        pltpu.make_async_copy(
            now_hbm, field.at[0, pl.ds(4, CX), pl.ds(8, CY), :], load_sem.at[0]
        ),
        pltpu.make_async_copy(
            prev_hbm, field.at[1, pl.ds(4, CX), pl.ds(8, CY), :], load_sem.at[1]
        ),
        pltpu.make_async_copy(courant_hbm, courant, load_sem.at[2]),
        pltpu.make_async_copy(forward_hbm, forward, load_sem.at[3]),
    ]
    for copy in loads:
        copy.start()

    @pl.when(gx == 0)
    def _():
        field[:, 0:4, 8 : 8 + CY, :] = jnp.zeros((2, 4, CY, NZ), F32)

    @pl.when(gx == NG - 1)
    def _():
        field[:, 12:16, 8 : 8 + CY, :] = jnp.zeros((2, 4, CY, NZ), F32)

    @pl.when(gy == 0)
    def _():
        field[:, 4:12, 0:8, :] = jnp.zeros((2, CX, 8, NZ), F32)

    @pl.when(gy == NYD - 1)
    def _():
        field[:, 4:12, 8 + CY : 16 + CY, :] = jnp.zeros((2, CX, 8, NZ), F32)

    barrier = pltpu.get_barrier_semaphore()

    def greet(k, carry):
        pl.semaphore_signal(
            barrier, inc=1, device_id={"gx": (gx + k) % NG}, device_id_type=MESH
        )
        return carry

    lax.fori_loop(1, NG, greet, 0)
    for k in (1, NYD - 1):
        pl.semaphore_signal(
            barrier, inc=1, device_id={"gy": (gy + k) % NYD}, device_id_type=MESH
        )

    for copy in small[:5]:
        copy.wait()

    rows = iota((BLOCKS, 128), 0)
    lanes = iota((BLOCKS, 128), 1)
    diagonal = rows == lanes
    slab_float = slab_ref[...].astype(F32)
    shot_row = shot_ref[...]
    cell_row = cell_ref[...].astype(F32)
    live_row = jnp.zeros((1, 128), F32)
    for s in range(SHOTS):
        flag = jnp.where(rollback_ref[s] == 0, 1.0, 0.0)
        live_row = jnp.where(shot_row == s, flag, live_row)
    live_col = jnp.sum(jnp.where(diagonal, live_row, 0.0), axis=1, keepdims=True)
    cell_col = jnp.sum(jnp.where(diagonal, cell_row, 0.0), axis=1, keepdims=True)
    slab_row = slab_float
    slab_col = jnp.sum(jnp.where(diagonal, slab_row, 0.0), axis=1, keepdims=True)
    slot_col = jnp.sum(
        jnp.where((slab_col == slab_row) & (lanes < rows), 1.0, 0.0), axis=1, keepdims=True
    )
    pick = jnp.where((lanes % 8 == rows // SAMPLES_PER_STEP) & (lanes < 8 * SLOTS), 1.0, 0.0)
    reduced = jnp.dot(traces_ref[0], pick, precision=HIGHEST, preferred_element_type=F32)
    entries = reduced * live_col + jnp.where(lanes % 8 == STEPS, cell_col, 0.0)
    entries = jnp.where(slot_col == (lanes // 8).astype(F32), entries, 0.0)
    named = jnp.where(iota((NG, BLOCKS), 0).astype(F32) == slab_row, 1.0, 0.0)
    packed[...] = jnp.dot(
        named, entries, precision=HIGHEST, preferred_element_type=F32
    ).reshape(NG, 1, 128)

    pl.semaphore_wait(barrier, NG - 1 + 2)

    def x_copies(parity, chunk, source_low, source_high):
        band = pl.ds(pl.multiple_of(8 + chunk * ROWS, 8), ROWS)
        low = pltpu.make_async_remote_copy(
            src_ref=source_low,
            dst_ref=field.at[parity, pl.ds(12, 4), band, :],
            send_sem=x_send.at[parity, 0, chunk],
            recv_sem=x_recv.at[parity, 1, chunk],
            device_id={"gx": (gx + NG - 1) % NG},
            device_id_type=MESH,
        )
        high = pltpu.make_async_remote_copy(
            src_ref=source_high,
            dst_ref=field.at[parity, pl.ds(0, 4), band, :],
            send_sem=x_send.at[parity, 1, chunk],
            recv_sem=x_recv.at[parity, 0, chunk],
            device_id={"gx": (gx + 1) % NG},
            device_id_type=MESH,
        )
        return low, high

    def x_field(parity, chunk):
        band = pl.ds(pl.multiple_of(8 + chunk * ROWS, 8), ROWS)
        return x_copies(
            parity, chunk, field.at[parity, pl.ds(4, 4), band, :], field.at[parity, pl.ds(8, 4), band, :]
        )

    def y_copies(parity, source_low, source_high):
        low = pltpu.make_async_remote_copy(
            src_ref=source_low,
            dst_ref=field.at[parity, pl.ds(4, CX), pl.ds(8 + CY, 8), :],
            send_sem=y_send.at[parity, 0],
            recv_sem=y_recv.at[parity, 1],
            device_id={"gy": (gy + NYD - 1) % NYD},
            device_id_type=MESH,
        )
        high = pltpu.make_async_remote_copy(
            src_ref=source_high,
            dst_ref=field.at[parity, pl.ds(4, CX), pl.ds(0, 8), :],
            send_sem=y_send.at[parity, 1],
            recv_sem=y_recv.at[parity, 0],
            device_id={"gy": (gy + 1) % NYD},
            device_id_type=MESH,
        )
        return low, high

    def y_field(parity):
        return y_copies(
            parity,
            field.at[parity, pl.ds(4, CX), pl.ds(8, 8), :],
            field.at[parity, pl.ds(4, CX), pl.ds(CY, 8), :],
        )

    has_low, has_high = gx > 0, gx < NG - 1
    y_has_low, y_has_high = gy > 0, gy < NYD - 1

    def order(i):
        return (CHUNKS - i) % CHUNKS

    now_low, now_high = y_copies(0, now_hbm.at[:, pl.ds(0, 8), :], now_hbm.at[:, pl.ds(CY - 8, 8), :])
    pl.when(y_has_low)(now_low.start)
    pl.when(y_has_high)(now_high.start)

    def send_now(i, carry):
        chunk = order(i)
        band = pl.ds(pl.multiple_of(chunk * ROWS, 8), ROWS)
        low, high = x_copies(
            0, chunk, now_hbm.at[pl.ds(0, 4), band, :], now_hbm.at[pl.ds(4, 4), band, :]
        )
        pl.when(has_low)(low.start)
        pl.when(has_high)(high.start)
        return carry

    def trace_copy(peer, mine):
        return pltpu.make_async_remote_copy(
            src_ref=packed.at[peer],
            dst_ref=landed.at[mine],
            send_sem=trace_send.at[peer],
            recv_sem=trace_recv.at[mine],
            device_id={"gx": peer},
            device_id_type=MESH,
        )

    def send_traces(k, carry):
        trace_copy((gx + k) % NG, gx).start()
        return carry

    lax.fori_loop(1, NG, send_traces, 0)
    lax.fori_loop(0, CHUNKS, send_now, 0)

    landed[gx] = packed[gx]

    def wait_traces(k, carry):
        peer = (gx + k) % NG
        trace_copy(peer, peer).wait_recv()
        return carry

    lax.fori_loop(1, NG, wait_traces, 0)

    def wait_trace_sends(k, carry):
        peer = (gx + k) % NG
        trace_copy(peer, peer).wait_send()
        return carry

    lax.fori_loop(1, NG, wait_trace_sends, 0)

    arrived = landed[...].reshape(NG, 128)
    lane = iota((NG, 128), 1)
    spread = jnp.zeros((CY, 128), F32)
    for j in range(SLOTS):
        cell = arrived[:, 8 * j + STEPS : 8 * j + STEPS + 1].astype(jnp.int32)
        weights = jnp.zeros((NG, 128), F32)
        for t in range(STEPS):
            weights = jnp.where(lane // CX == t, arrived[:, 8 * j + t : 8 * j + t + 1], weights)
        weights = jnp.where(lane % CX == cell // CY, weights, 0.0)
        spot = jnp.where(lane == cell % CY, 1.0, 0.0)
        spread = spread + lax.dot_general(
            spot, weights, (((0,), (0,)), ((), ())), precision=HIGHEST, preferred_element_type=F32
        )
    at_depth = iota((CY, 128), 1) == ZREC
    for c in range(STEPS * CX):
        source[c] = jnp.where(at_depth, spread[:, c : c + 1], 0.0)

    for copy in loads + small[5:]:
        copy.wait()

    eight = iota((8, NZ), 0)

    def advance(t):
        now, later = t % 2, (t + 1) % 2

        def chunk_body(i, carry):
            chunk = order(i)
            low, high = x_field(now, chunk)
            pl.when(has_low)(high.wait_recv)
            pl.when(has_high)(low.wait_recv)
            if t >= 1:
                old_low, old_high = x_field(later, chunk)
                pl.when(has_low)(old_low.wait_send)
                pl.when(has_high)(old_high.wait_send)

            @pl.when(i == 0)
            def _():
                y_low, y_high = y_field(now)
                pl.when(y_has_low)(y_high.wait_recv)
                pl.when(y_has_high)(y_low.wait_recv)
                if t >= 1:
                    y_old_low, y_old_high = y_field(later)
                    pl.when(y_has_low)(y_old_low.wait_send)
                    pl.when(y_has_high)(y_old_high.wait_send)

            base = pl.multiple_of(chunk * ROWS, ROWS)
            depth[...] = jnp.dot(
                field[now, 4:12, pl.ds(base + 8, ROWS), :].reshape(CX * ROWS, NZ),
                table_ref[...],
                precision=HIGHEST,
                preferred_element_type=F32,
            ).reshape(CX, ROWS, NZ)

            def row_body(j, carry):
                top = pl.multiple_of(base + j * 16, 16)
                for x in range(CX):
                    wave = forward[t, x, pl.ds(top, 16), :].astype(F32)
                    for half in range(2):
                        inner = pl.multiple_of(j * 16 + half * 8, 8)
                        row = pl.multiple_of(top + half * 8, 8)
                        r = pl.ds(pl.multiple_of(row + 8, 8), 8)
                        mid = field[now, 4 + x, r, :]
                        above = field[now, 4 + x, pl.ds(row, 8), :]
                        below = field[now, 4 + x, pl.ds(pl.multiple_of(row + 16, 8), 8), :]
                        total_sum = depth[x, pl.ds(inner, 8), :]
                        for k, w in enumerate(coefficients, 1):
                            paired = field[now, 4 + x + k, r, :] + field[now, 4 + x - k, r, :]
                            paired += pltpu.roll(jnp.where(eight >= k, mid, below), 8 - k, 0)
                            paired += pltpu.roll(jnp.where(eight < 8 - k, mid, above), k, 0)
                            total_sum += w * paired
                        out_rows = pl.ds(row, 8)
                        following = (
                            2.0 * mid
                            - field[later, 4 + x, r, :]
                            + courant[x, out_rows, :] * total_sum
                        )
                        following = jnp.concatenate(
                            [
                                following[:, :128] + source[t * CX + x, out_rows, :],
                                following[:, 128:],
                            ],
                            axis=1,
                        )
                        field[later, 4 + x, r, :] = following
                        term = wave[half * 8 : half * 8 + 8] * following
                        if t == 0:
                            image[x, out_rows, :] = term
                        else:
                            image[x, out_rows, :] += term
                return carry

            lax.fori_loop(0, ROWS // 16, row_body, 0)

            if t < STEPS - 1:
                next_low, next_high = x_field(later, chunk)
                pl.when(has_low)(next_low.start)
                pl.when(has_high)(next_high.start)

                y_low, y_high = y_field(later)

                @pl.when(i == 0)
                def _():
                    pl.when(y_has_low)(y_low.start)

                @pl.when(i == 1)
                def _():
                    pl.when(y_has_high)(y_high.start)

            return carry

        lax.fori_loop(0, CHUNKS, chunk_body, 0)

    for t in range(STEPS):
        advance(t)

    store_last = pltpu.make_async_copy(
        field.at[STEPS % 2, pl.ds(4, CX), pl.ds(8, CY), :], last_hbm, store_sem.at[0]
    )
    store_image = pltpu.make_async_copy(image, image_hbm, store_sem.at[1])
    store_last.start()
    store_image.start()

    def weigh(j, carry):
        r = pl.ds(pl.multiple_of(j * 8, 8), 8)
        up = jnp.zeros((8, NZ), F32)
        down = jnp.zeros((8, NZ), F32)
        for x in range(CX):
            value = image[x, r, :]
            up += factor_ref[gx * CX + x] * value
            down += factor_ref[NG * CX + gx * CX + x] * value
        plane[0, r, :] = up
        plane[1, r, :] = down
        return carry

    lax.fori_loop(0, CY // 8, weigh, 0)

    def segment(q):
        return pl.ds(pl.multiple_of(q * SEG, SEG), SEG)

    def group_copy(peer, mine):
        return pltpu.make_async_remote_copy(
            src_ref=plane.at[:, segment(peer), :],
            dst_ref=group_in.at[mine],
            send_sem=group_send.at[peer],
            recv_sem=group_recv.at[mine],
            device_id={"gx": own_z * NQ + peer},
            device_id_type=MESH,
        )

    def line_copy(k):
        peer = (own_z + k) % NZD
        return pltpu.make_async_remote_copy(
            src_ref=total.at[(own_z + k) // NZD],
            dst_ref=line_in.at[own_z],
            send_sem=line_send.at[peer],
            recv_sem=line_recv.at[own_z],
            device_id={"gx": peer * NQ + own_q},
            device_id_type=MESH,
        )

    def line_arrival(k):
        peer = (own_z + k) % NZD
        return pltpu.make_async_remote_copy(
            src_ref=total.at[0],
            dst_ref=line_in.at[peer],
            send_sem=line_send.at[peer],
            recv_sem=line_recv.at[peer],
            device_id={"gx": peer * NQ + own_q},
            device_id_type=MESH,
        )

    def back_copy(peer, mine):
        return pltpu.make_async_remote_copy(
            src_ref=back.at[peer],
            dst_ref=sums.at[:, segment(mine), :],
            send_sem=back_send.at[peer],
            recv_sem=back_recv.at[mine],
            device_id={"gx": own_z * NQ + peer},
            device_id_type=MESH,
        )

    for k in range(1, NQ):
        group_copy((own_q + k) % NQ, own_q).start()
    group_in[own_q] = plane[:, segment(own_q), :]
    for k in range(1, NQ):
        peer = (own_q + k) % NQ
        group_copy(peer, peer).wait_recv()

    below_sum = group_in[0, 0]
    above_sum = group_in[NQ - 1, 1]
    for q in range(1, NQ):
        below_sum = below_sum + group_in[q, 0]
        above_sum = above_sum + group_in[NQ - 1 - q, 1]
    total[0] = below_sum
    total[1] = above_sum

    for k in range(1, NZD):
        line_copy(k).start()
    line_in[own_z] = jnp.zeros((SEG, NZ), F32)
    for k in range(1, NZD):
        line_arrival(k).wait_recv()

    low_sum = jnp.zeros((SEG, NZ), F32)
    high_sum = jnp.zeros((SEG, NZ), F32)
    for z in range(NZD):
        part = line_in[z]
        low_sum = low_sum + jnp.where(z < own_z, part, 0.0)
        high_sum = high_sum + jnp.where(z > own_z, part, 0.0)
    for q in range(NQ):
        back[q, 0] = low_sum
        low_sum = low_sum + group_in[q, 0]
        back[NQ - 1 - q, 1] = high_sum
        high_sum = high_sum + group_in[NQ - 1 - q, 1]

    for k in range(1, NQ):
        back_copy((own_q + k) % NQ, own_q).start()
    sums[:, segment(own_q), :] = back[own_q]
    for k in range(1, NQ):
        peer = (own_q + k) % NQ
        back_copy(peer, peer).wait_recv()

    store_sums = pltpu.make_async_copy(sums, sums_hbm, store_sem.at[2])
    store_sums.start()

    for k in range(1, NQ):
        peer = (own_q + k) % NQ
        group_copy(peer, peer).wait_send()
        back_copy(peer, peer).wait_send()
    for k in range(1, NZD):
        line_arrival(k).wait_send()
    def wait_sends(i, carry):
        low, high = x_field((STEPS - 1) % 2, i)
        pl.when(has_low)(low.wait_send)
        pl.when(has_high)(high.wait_send)
        return carry

    lax.fori_loop(0, CHUNKS, wait_sends, 0)
    low, high = y_field((STEPS - 1) % 2)
    pl.when(y_has_low)(low.wait_send)
    pl.when(y_has_high)(high.wait_send)
    store_last.wait()
    store_image.wait()
    store_sums.wait()


def update_kernel(
    factor_ref,
    image_ref,
    sums_ref,
    last_ref,
    courant_ref,
    first_ref,
    second_ref,
    courant_out,
    first_out,
    second_out,
    last_out,
    fresh,
    store_sem,
):
    gx = lax.axis_index("gx")
    store_last = pltpu.make_async_copy(last_ref, last_out, store_sem.at[3, 0])
    store_last.start()
    rise = [factor_ref[gx * CX + x] for x in range(CX)]
    fall = [factor_ref[NG * CX + gx * CX + x] for x in range(CX)]

    def stores(part):
        band = pl.ds(part * UPDATE_ROWS, UPDATE_ROWS)
        return [
            pltpu.make_async_copy(fresh.at[k, :, band, :], out.at[:, band, :], store_sem.at[k, part])
            for k, out in enumerate((courant_out, first_out, second_out))
        ]

    for part in range(CY // UPDATE_ROWS):

        def body(j, carry):
            r = pl.ds(pl.multiple_of(part * UPDATE_ROWS + j * 8, 8), 8)
            low = sums_ref[0, r, :]
            high = sums_ref[1, r, :]
            values = [image_ref[x, r, :] for x in range(CX)]
            below = []
            for x in range(CX):
                low = low + rise[x] * values[x]
                below.append(low)
            for x in reversed(range(CX)):
                smoothed = fall[x] * below[x] + rise[x] * high
                high = high + fall[x] * values[x]
                first = beta_first * first_ref[x, r, :] + (1.0 - beta_first) * smoothed
                second = beta_second * second_ref[x, r, :] + (1.0 - beta_second) * smoothed * smoothed
                fresh[1, x, r, :] = first
                fresh[2, x, r, :] = second
                fresh[0, x, r, :] = courant_ref[x, r, :] - learning_rate * (first / bias_first) / (
                    jnp.sqrt(second / bias_second) + epsilon
                )
            return carry

        lax.fori_loop(0, UPDATE_ROWS // 8, body, 0)
        for copy in stores(part):
            copy.start()
    for part in range(CY // UPDATE_ROWS):
        for copy in stores(part):
            copy.wait()
    store_last.wait()


def shards(
    courant,
    first_moment,
    second_moment,
    adjoint_prev,
    adjoint_now,
    forward_field,
    traces,
    trace_slab,
    trace_cell,
    trace_shot,
    rollback,
):
    factors = jnp.asarray(smoother_factors(NG * CX))
    table = jnp.asarray(depth_table())
    shape = jax.ShapeDtypeStruct((CX, CY, NZ), F32)
    anywhere = pl.BlockSpec(memory_space=pl.ANY)
    hbm = pl.BlockSpec(memory_space=pltpu.HBM)
    smem = pl.BlockSpec(memory_space=pltpu.SMEM)
    vmem = pl.BlockSpec(memory_space=pltpu.VMEM)
    dma = pltpu.SemaphoreType.DMA
    image, last, sums = pl.pallas_call(
        window_kernel,
        out_shape=(shape, shape, jax.ShapeDtypeStruct((2, CY, NZ), F32)),
        in_specs=[hbm] * 11,
        out_specs=(anywhere,) * 3,
        scratch_shapes=[
            pltpu.SMEM((SHOTS,), jnp.int32),
            pltpu.SMEM((2 * NG * CX,), F32),
            pltpu.VMEM((NZ, NZ), F32),
            pltpu.VMEM((1, BLOCKS, 128), F32),
            pltpu.VMEM((1, BLOCKS), jnp.int32),
            pltpu.VMEM((1, BLOCKS), jnp.int32),
            pltpu.VMEM((1, BLOCKS), jnp.int32),
            pltpu.VMEM((2, CX + 8, CY + 16, NZ), F32),
            pltpu.VMEM((CX, CY, NZ), F32),
            pltpu.VMEM((STEPS, CX, CY, NZ), jnp.bfloat16),
            pltpu.VMEM((CX, CY, NZ), F32),
            pltpu.VMEM((STEPS * CX, CY, 128), F32),
            pltpu.VMEM((NG, 1, 128), F32),
            pltpu.VMEM((NG, 1, 128), F32),
            pltpu.VMEM((CX, ROWS, NZ), F32),
            pltpu.VMEM((2, CY, NZ), F32),
            pltpu.VMEM((NQ, 2, SEG, NZ), F32),
            pltpu.VMEM((2, SEG, NZ), F32),
            pltpu.VMEM((NZD, SEG, NZ), F32),
            pltpu.VMEM((NQ, 2, SEG, NZ), F32),
            pltpu.VMEM((2, CY, NZ), F32),
            dma((11,)),
            dma((NG,)),
            dma((NG,)),
            dma((2, 2, CHUNKS)),
            dma((2, 2, CHUNKS)),
            dma((2, 2)),
            dma((2, 2)),
            dma((NQ,)),
            dma((NQ,)),
            dma((NZD,)),
            dma((NZD,)),
            dma((NQ,)),
            dma((NQ,)),
            dma((3,)),
        ],
        compiler_params=pltpu.CompilerParams(
            collective_id=0, has_side_effects=True, vmem_limit_bytes=24 << 20
        ),
    )(
        *(
            pltpu.with_memory_space_constraint(operand, pltpu.HBM)
            for operand in (
                rollback,
                factors,
                table,
                traces,
                trace_slab.reshape(1, BLOCKS),
                trace_cell,
                trace_shot,
                courant,
                adjoint_prev,
                adjoint_now,
                forward_field,
            )
        )
    )

    return pl.pallas_call(
        update_kernel,
        out_shape=(shape,) * 4,
        in_specs=[smem] + [vmem] * 6,
        out_specs=(anywhere,) * 4,
        scratch_shapes=[pltpu.VMEM((3, CX, CY, NZ), F32), dma((4, CY // UPDATE_ROWS))],
        compiler_params=pltpu.CompilerParams(vmem_limit_bytes=24 << 20),
    )(factors, image, sums, last, courant, first_moment, second_moment)


def solution(mesh):
    in_specs = (
        P("gx", "gy", None),
        P("gx", "gy", None),
        P("gx", "gy", None),
        P("gx", "gy", None),
        P("gx", "gy", None),
        P(None, "gx", "gy", None),
        P("gy", "gx", None),
        P("gy", "gx", None),
        P("gy", "gx"),
        P("gy", "gx"),
        P(),
    )
    out_specs = (P("gx", "gy", None),) * 4
    return jax.shard_map(shards, mesh=mesh, in_specs=in_specs, out_specs=out_specs, check_vma=False)
```

```python
import math

import jax
import jax.numpy as jnp
import numpy as np
from jax import lax
from jax.experimental import pallas as pl
from jax.experimental.pallas import tpu as pltpu
from jax.sharding import PartitionSpec as P

MESH = pl.DeviceIdType.MESH
F32 = jnp.float32
HIGHEST = lax.Precision.HIGHEST

STEPS = 4
SAMPLES_PER_STEP = 32
ZREC = 8
SHOTS = 16
NG = 64
NYD = 4
NQ = 8
NZD = 8
CX, CY, NZ = 8, 128, 256
BLOCKS = 128
SLOTS = 4
ROWS = 16
CHUNKS = CY // ROWS
GROUP = 32 // ROWS
BATCHES = CHUNKS // GROUP
PASS_AFTER = 2
FAR_FIRST = (4, 3, 5, 2, 6, 7, 1)
UPDATE_ROWS = 32

coefficients = (8.0 / 5.0, -1.0 / 5.0, 8.0 / 315.0, -1.0 / 560.0)
center_weight = -205.0 / 72.0
smooth_length = 4096.0
cosh_value = 1.0 + 0.5 / smooth_length
theta = math.log(cosh_value + math.sqrt(cosh_value * cosh_value - 1.0))
image_gain = 10.0
beta_first = 0.9
beta_second = 0.999
bias_first = 1.0 - 0.9**10
bias_second = 1.0 - 0.999**10
learning_rate = 0.01
epsilon = 1e-08


def depth_table():
    table = np.zeros((NZ, NZ), np.float64)
    for i in range(NZ):
        for k, w in enumerate(coefficients, 1):
            if i + k < NZ:
                table[i + k, i] = w
                table[i, i + k] = w
    table = jnp.asarray(table.astype(np.float32))
    high = table.astype(jnp.bfloat16)
    return jnp.stack([high, (table - high.astype(F32)).astype(jnp.bfloat16)])


def smoother_factors(count):
    position = np.arange(count, dtype=np.float64)
    scale = math.sqrt(image_gain / (smooth_length * math.sinh(theta) * math.sinh(theta * (count + 1))))
    rise = scale * np.sinh(theta * (position + 1.0))
    fall = scale * np.sinh(theta * (count - position))
    return np.concatenate([rise, fall]).astype(np.float32)


def iota(shape, dim):
    return lax.broadcasted_iota(jnp.int32, shape, dim)


def window_kernel(
    rollback_hbm,
    factor_hbm,
    table_hbm,
    traces_hbm,
    slab_hbm,
    cell_hbm,
    shot_hbm,
    courant_hbm,
    prev_hbm,
    now_hbm,
    forward_hbm,
    image_hbm,
    last_hbm,
    sums_hbm,
    rollback_ref,
    factor_ref,
    table_ref,
    traces_ref,
    slab_ref,
    cell_ref,
    shot_ref,
    field,
    courant,
    forward,
    image,
    source,
    packed,
    passed,
    landed,
    depth,
    plane,
    group_in,
    total,
    line_in,
    back,
    load_sem,
    known_sem,
    pack_send,
    pack_recv,
    pass_send,
    pass_recv,
    x_send,
    x_recv,
    y_send,
    y_recv,
    x_half_send,
    x_half_recv,
    y_half_send,
    y_half_recv,
    group_send,
    group_recv,
    line_send,
    line_recv,
    back_send,
    back_recv,
    store_sem,
):
    gx = lax.axis_index("gx")
    gy = lax.axis_index("gy")
    own_z = gx // NQ
    own_q = gx % NQ

    def at_group(q):
        return {"gx": own_z * NQ + q}

    def at_line(z):
        return {"gx": z * NQ + own_q}

    def remote(source_ref, target_ref, send_sem, recv_sem, device):
        return pltpu.make_async_remote_copy(
            src_ref=source_ref,
            dst_ref=target_ref,
            send_sem=send_sem,
            recv_sem=recv_sem,
            device_id=device,
            device_id_type=MESH,
        )

    def signal(sem, device):
        pl.semaphore_signal(sem, inc=1, device_id=device, device_id_type=MESH)

    barrier = pltpu.get_barrier_semaphore()
    at_edge = own_q % (NQ - 1) == 0
    for k in range(1, NQ):
        signal(barrier, at_group((own_q + k) % NQ))
    for k in (1, NYD - 1):
        signal(barrier, {"gy": (gy + k) % NYD})
    for k in (1, NZD - 1):
        signal(barrier, at_line((own_z + k) % NZD))
    across = (gx + 1 - 2 * ((NQ - 1 - own_q) // (NQ - 1)) + NG) % NG

    @pl.when(at_edge)
    def _():
        signal(barrier, {"gx": across})

    small = [
        pltpu.make_async_copy(source_ref, target_ref, load_sem.at[4 + k])
        for k, (source_ref, target_ref) in enumerate(
            (
                (traces_hbm, traces_ref),
                (slab_hbm, slab_ref),
                (cell_hbm, cell_ref),
                (shot_hbm, shot_ref),
                (rollback_hbm, rollback_ref),
                (table_hbm, table_ref),
                (factor_hbm, factor_ref),
            )
        )
    ]
    for copy in small:
        copy.start()
    loads = [
        pltpu.make_async_copy(
            now_hbm, field.at[0, pl.ds(4, CX), pl.ds(8, CY), :], load_sem.at[0]
        ),
        pltpu.make_async_copy(
            prev_hbm, field.at[1, pl.ds(4, CX), pl.ds(8, CY), :], load_sem.at[1]
        ),
        pltpu.make_async_copy(courant_hbm, courant, load_sem.at[2]),
        pltpu.make_async_copy(forward_hbm, forward, load_sem.at[3]),
    ]
    for copy in loads:
        copy.start()

    @pl.when(gx == 0)
    def _():
        field[:, 0:4, 8 : 8 + CY, :] = jnp.zeros((2, 4, CY, NZ), F32)

    @pl.when(gx == NG - 1)
    def _():
        field[:, 12:16, 8 : 8 + CY, :] = jnp.zeros((2, 4, CY, NZ), F32)

    @pl.when(gy == 0)
    def _():
        field[:, 4:12, 0:8, :] = jnp.zeros((2, CX, 8, NZ), F32)

    @pl.when(gy == NYD - 1)
    def _():
        field[:, 4:12, 8 + CY : 16 + CY, :] = jnp.zeros((2, CX, 8, NZ), F32)

    pl.semaphore_wait(barrier, NQ - 1 + 4 + 1 - (own_q % (NQ - 1) + NQ - 2) // (NQ - 1))

    has_low, has_high = gx > 0, gx < NG - 1
    y_has_low, y_has_high = gy > 0, gy < NYD - 1
    x_low = {"gx": (gx + NG - 1) % NG}
    x_high = {"gx": (gx + 1) % NG}
    y_low = {"gy": (gy + NYD - 1) % NYD}
    y_high = {"gy": (gy + 1) % NYD}
    every = pl.ds(0, NZ)

    def order(i):
        return (CHUNKS - i) % CHUNKS

    def band_of(chunk, start):
        return pl.ds(pl.multiple_of(start + chunk * ROWS, 8), ROWS)

    def x_pair(parity, chunk, sources, lanes, send, recv):
        band = band_of(chunk, 8)
        low = remote(
            sources[0], field.at[parity, pl.ds(12, 4), band, lanes], send(0), recv(1), x_low
        )
        high = remote(
            sources[1], field.at[parity, pl.ds(0, 4), band, lanes], send(1), recv(0), x_high
        )
        return low, high

    def x_field(parity, chunk, half=None):
        band = band_of(chunk, 8)
        if half is None:
            lanes = every
            send = lambda side: x_send.at[parity, side, chunk]
            recv = lambda side: x_recv.at[parity, side, chunk]
        else:
            lanes = pl.ds(half * 128, 128)
            send = lambda side: x_half_send.at[half, side, chunk]
            recv = lambda side: x_half_recv.at[half, side, chunk]
        sources = (
            field.at[parity, pl.ds(4, 4), band, lanes],
            field.at[parity, pl.ds(8, 4), band, lanes],
        )
        return x_pair(parity, chunk, sources, lanes, send, recv)

    def y_pair(parity, sources, lanes, send, recv):
        low = remote(
            sources[0],
            field.at[parity, pl.ds(4, CX), pl.ds(8 + CY, 8), lanes],
            send(0),
            recv(1),
            y_low,
        )
        high = remote(
            sources[1], field.at[parity, pl.ds(4, CX), pl.ds(0, 8), lanes], send(1), recv(0), y_high
        )
        return low, high

    def y_field(parity, half=None):
        if half is None:
            lanes = every
            send = lambda side: y_send.at[parity, side]
            recv = lambda side: y_recv.at[parity, side]
        else:
            lanes = pl.ds(half * 128, 128)
            send = lambda side: y_half_send.at[half, side]
            recv = lambda side: y_half_recv.at[half, side]
        sources = (
            field.at[parity, pl.ds(4, CX), pl.ds(8, 8), lanes],
            field.at[parity, pl.ds(4, CX), pl.ds(CY, 8), lanes],
        )
        return y_pair(parity, sources, lanes, send, recv)

    low, high = y_pair(
        0,
        (now_hbm.at[:, pl.ds(0, 8), :], now_hbm.at[:, pl.ds(CY - 8, 8), :]),
        every,
        lambda side: y_send.at[0, side],
        lambda side: y_recv.at[0, side],
    )
    pl.when(y_has_low)(low.start)
    pl.when(y_has_high)(high.start)

    def send_now(i, carry):
        chunk = order(i)
        band = band_of(chunk, 0)
        low, high = x_pair(
            0,
            chunk,
            (now_hbm.at[pl.ds(0, 4), band, :], now_hbm.at[pl.ds(4, 4), band, :]),
            every,
            lambda side: x_send.at[0, side, chunk],
            lambda side: x_recv.at[0, side, chunk],
        )
        pl.when(has_low)(low.start)
        pl.when(has_high)(high.start)
        return carry

    send_now(0, 0)

    line_next = at_line((own_z + 1) % NZD)
    line_prev = at_line((own_z + NZD - 1) % NZD)
    signal(known_sem.at[0, 0], line_next)
    signal(known_sem.at[1, 0], line_prev)

    for copy in small[:5]:
        copy.wait()
    rows = iota((BLOCKS, 128), 0)
    lanes = iota((BLOCKS, 128), 1)
    diagonal = rows == lanes
    slab_row = slab_ref[...].astype(F32)
    shot_row = shot_ref[...]
    cell_row = cell_ref[...].astype(F32)
    live_row = jnp.zeros((1, 128), F32)
    for s in range(SHOTS):
        flag = jnp.where(rollback_ref[s] == 0, 1.0, 0.0)
        live_row = jnp.where(shot_row == s, flag, live_row)
    live_col = jnp.sum(jnp.where(diagonal, live_row, 0.0), axis=1, keepdims=True)
    cell_col = jnp.sum(jnp.where(diagonal, cell_row, 0.0), axis=1, keepdims=True)
    slab_col = jnp.sum(jnp.where(diagonal, slab_row, 0.0), axis=1, keepdims=True)
    slot_col = jnp.sum(
        jnp.where((slab_col == slab_row) & (lanes < rows), 1.0, 0.0), axis=1, keepdims=True
    )
    pick = jnp.where((lanes % 8 == rows // SAMPLES_PER_STEP) & (lanes < 8 * SLOTS), 1.0, 0.0)
    reduced = jnp.dot(traces_ref[0], pick, precision=HIGHEST, preferred_element_type=F32)
    entries = reduced * live_col + jnp.where(lanes % 8 == STEPS, cell_col, 0.0)
    entries = jnp.where(slot_col == (lanes // 8).astype(F32), entries, 0.0)
    row = iota((NG, BLOCKS), 0)
    row_slab = (row % NZD) * NQ + row // NZD
    named = jnp.where(row_slab.astype(F32) == slab_row, 1.0, 0.0)
    packed[...] = jnp.dot(
        named, entries, precision=HIGHEST, preferred_element_type=F32
    ).reshape(NQ, NZD, 1, 128)

    def pack_copy(peer, mine):
        return remote(
            packed.at[peer], passed.at[mine], pack_send.at[peer], pack_recv.at[mine], at_group(peer)
        )

    def pass_copy(peer, mine):
        return remote(
            passed.at[:, peer], landed.at[mine], pass_send.at[peer], pass_recv.at[mine], at_line(peer)
        )

    for k in FAR_FIRST:
        pack_copy((own_q + k) % NQ, own_q).start()
    lax.fori_loop(1, CHUNKS, send_now, 0)
    passed[own_q] = packed[own_q]

    pl.semaphore_wait(known_sem.at[0, 0], 1)
    signal(known_sem.at[0, 1], line_next)
    pl.semaphore_wait(known_sem.at[1, 0], 1)
    signal(known_sem.at[1, 1], line_prev)
    pl.semaphore_wait(known_sem.at[0, 1], 1)
    signal(known_sem.at[0, 2], line_next)
    pl.semaphore_wait(known_sem.at[1, 1], 1)
    pl.semaphore_wait(known_sem.at[0, 2], 1)

    def pass_on():
        for k in range(1, NQ):
            peer = (own_q + k) % NQ
            pack_copy(peer, peer).wait_recv()
        for k in FAR_FIRST:
            pass_copy((own_z + k) % NZD, own_z).start()
        landed[own_z] = passed[:, own_z]

    for copy in loads + small[5:]:
        copy.wait()

    eight = iota((8, NZ), 0)
    at_depth = iota((8, 128), 1) == ZREC
    rise = [factor_ref[gx * CX + x] for x in range(CX)]
    fall = [factor_ref[NG * CX + gx * CX + x] for x in range(CX)]

    def group_copy(chunk, peer, mine):
        return remote(
            plane.at[chunk, peer],
            group_in.at[chunk, mine],
            group_send.at[chunk, peer],
            group_recv.at[chunk, mine],
            at_group(peer),
        )

    def line_copy(chunk, k):
        peer = (own_z + k) % NZD
        return remote(
            total.at[chunk, (own_z + k) // NZD],
            line_in.at[chunk, own_z],
            line_send.at[chunk, peer],
            line_recv.at[chunk, own_z],
            at_line(peer),
        )

    def line_arrival(chunk, k):
        peer = (own_z + k) % NZD
        return remote(
            total.at[chunk, 0],
            line_in.at[chunk, peer],
            line_send.at[chunk, peer],
            line_recv.at[chunk, peer],
            at_line(peer),
        )

    def back_copy(chunk, peer, mine):
        return remote(
            back.at[chunk, peer],
            sums_hbm.at[chunk, mine],
            back_send.at[chunk, peer],
            back_recv.at[chunk, mine],
            at_group(peer),
        )

    def wait_x(parity, chunk, half, what):
        low, high = x_field(parity, chunk, half)
        if what == "recv":
            pl.when(has_low)(high.wait_recv)
            pl.when(has_high)(low.wait_recv)
        else:
            pl.when(has_low)(low.wait_send)
            pl.when(has_high)(high.wait_send)

    def wait_y(parity, half, what):
        low, high = y_field(parity, half)
        if what == "recv":
            pl.when(y_has_low)(high.wait_recv)
            pl.when(y_has_high)(low.wait_recv)
        else:
            pl.when(y_has_low)(low.wait_send)
            pl.when(y_has_high)(high.wait_send)

    def parts(parity, sent_at):
        return (0, 1) if sent_at == 0 else (None,)

    def send_halo(i, chunk, parity, half):
        low, high = x_field(parity, chunk, half)
        pl.when(has_low)(low.start)
        pl.when(has_high)(high.start)
        low, high = y_field(parity, half)

        @pl.when((i == 0) & y_has_low)
        def _():
            low.start()

        @pl.when((i == 1) & y_has_high)
        def _():
            high.start()

    def advance(t):
        now, later = t % 2, (t + 1) % 2

        def chunk_body(i, carry):
            chunk = order(i)
            for half in parts(now, t - 1):
                wait_x(now, chunk, half, "recv")
            if t >= 1:
                for half in parts(later, t - 2):
                    wait_x(later, chunk, half, "send")

            @pl.when(i == 0)
            def _():
                for half in parts(now, t - 1):
                    wait_y(now, half, "recv")
                if t >= 1:
                    for half in parts(later, t - 2):
                        wait_y(later, half, "send")

            base = pl.multiple_of(chunk * ROWS, ROWS)
            waves = field[now, 4:12, pl.ds(base + 8, ROWS), :].reshape(CX * ROWS, NZ)
            wave_high = waves.astype(jnp.bfloat16)
            wave_low = (waves - wave_high.astype(F32)).astype(jnp.bfloat16)
            depth[...] = (
                jnp.dot(wave_low, table_ref[0], preferred_element_type=F32)
                + jnp.dot(wave_high, table_ref[1], preferred_element_type=F32)
                + jnp.dot(wave_high, table_ref[0], preferred_element_type=F32)
            ).reshape(CX, ROWS, NZ)

            def row_body(j, carry):
                top = pl.multiple_of(base + j * 16, 16)
                up = [jnp.zeros((8, NZ), F32)] * 2
                down = [jnp.zeros((8, NZ), F32)] * 2
                for x in range(CX):
                    wave = forward[t, x, pl.ds(top, 16), :].astype(F32)
                    for half in range(2):
                        inner = pl.multiple_of(j * 16 + half * 8, 8)
                        row = pl.multiple_of(top + half * 8, 8)
                        r = pl.ds(pl.multiple_of(row + 8, 8), 8)
                        mid = field[now, 4 + x, r, :]
                        above = field[now, 4 + x, pl.ds(row, 8), :]
                        below = field[now, 4 + x, pl.ds(pl.multiple_of(row + 16, 8), 8), :]
                        total_sum = depth[x, pl.ds(inner, 8), :] + 3.0 * center_weight * mid
                        for k, w in enumerate(coefficients, 1):
                            paired = field[now, 4 + x + k, r, :] + field[now, 4 + x - k, r, :]
                            paired += pltpu.roll(jnp.where(eight >= k, mid, below), 8 - k, 0)
                            paired += pltpu.roll(jnp.where(eight < 8 - k, mid, above), k, 0)
                            total_sum += w * paired
                        out_rows = pl.ds(row, 8)
                        following = (
                            2.0 * mid
                            - field[later, 4 + x, r, :]
                            + courant[x, out_rows, :] * total_sum
                        )
                        if t > 0:
                            following = jnp.concatenate(
                                [
                                    following[:, :128]
                                    + jnp.where(
                                        at_depth,
                                        pltpu.roll(
                                            source[out_rows, :], (ZREC - t * CX - x) % 128, 1
                                        ),
                                        0.0,
                                    ),
                                    following[:, 128:],
                                ],
                                axis=1,
                            )
                        field[later, 4 + x, r, :] = following
                        value = wave[half * 8 : half * 8 + 8] * following
                        if t > 0:
                            value += image[x, out_rows, :]
                        image[x, out_rows, :] = value
                        if t == STEPS - 1:
                            up[half] = up[half] + rise[x] * value
                            down[half] = down[half] + fall[x] * value
                if t == STEPS - 1:
                    for half in range(2):
                        for side in range(2):
                            q = (i % GROUP) * (NQ // GROUP) + j * 4 + half * 2 + side
                            plane[i // GROUP, q, 0] = up[half][:, side * 128 : side * 128 + 128]
                            plane[i // GROUP, q, 1] = down[half][:, side * 128 : side * 128 + 128]
                return carry

            lax.fori_loop(0, ROWS // 16, row_body, 0)

            if t == 0:
                send_halo(i, chunk, later, 1)
                pl.when(i == PASS_AFTER)(pass_on)
            elif t < STEPS - 1:
                send_halo(i, chunk, later, None)
            else:
                batch = i // GROUP

                @pl.when(i % GROUP == GROUP - 1)
                def _():
                    for k in FAR_FIRST:
                        group_copy(batch, (own_q + k) % NQ, own_q).start()
                    group_in[batch, own_q] = plane[batch, own_q]

            return carry

        lax.fori_loop(0, CHUNKS, chunk_body, 0)

    advance(0)

    for k in range(1, NZD):
        peer = (own_z + k) % NZD
        pass_copy(peer, peer).wait_recv()
    arrived = landed[...].reshape(NG, 128)
    lane = iota((NG, 128), 1)
    spread = jnp.zeros((CY, 128), F32)
    for j in range(SLOTS):
        cell = arrived[:, 8 * j + STEPS : 8 * j + STEPS + 1].astype(jnp.int32)
        weights = jnp.zeros((NG, 128), F32)
        for t in range(STEPS):
            weights = jnp.where(lane // CX == t, arrived[:, 8 * j + t : 8 * j + t + 1], weights)
        weights = jnp.where(lane % CX == cell // CY, weights, 0.0)
        spot = jnp.where(lane == cell % CY, 1.0, 0.0)
        spread = spread + lax.dot_general(
            spot, weights, (((0,), (0,)), ((), ())), precision=HIGHEST, preferred_element_type=F32
        )
    source[...] = spread

    def inject(i, carry):
        chunk = order(i)
        out_rows = band_of(chunk, 0)
        in_rows = band_of(chunk, 8)
        packed_rows = source[out_rows, :]
        at_depth = iota((ROWS, 128), 1) == ZREC
        for x in range(CX):
            added = jnp.where(at_depth, pltpu.roll(packed_rows, (ZREC - x) % 128, 1), 0.0)
            wave = forward[0, x, out_rows, 0:128].astype(F32)
            field[1, 4 + x, in_rows, 0:128] += added
            image[x, out_rows, 0:128] += wave * added
        send_halo(i, chunk, 1, 0)
        return carry

    lax.fori_loop(0, CHUNKS, inject, 0)

    for t in range(1, STEPS):
        advance(t)

    store_last = pltpu.make_async_copy(
        field.at[STEPS % 2, pl.ds(4, CX), pl.ds(8, CY), :], last_hbm, store_sem.at[0]
    )
    store_image = pltpu.make_async_copy(image, image_hbm, store_sem.at[1])
    store_last.start()
    store_image.start()

    def reduce_group(batch, carry):
        for k in range(1, NQ):
            peer = (own_q + k) % NQ
            group_copy(batch, peer, peer).wait_recv()
        below_sum = group_in[batch, 0, 0]
        above_sum = group_in[batch, NQ - 1, 1]
        for q in range(1, NQ):
            below_sum = below_sum + group_in[batch, q, 0]
            above_sum = above_sum + group_in[batch, NQ - 1 - q, 1]
        total[batch, 0] = below_sum
        total[batch, 1] = above_sum
        for k in FAR_FIRST:
            line_copy(batch, k).start()
        line_in[batch, own_z] = jnp.zeros((8, 128), F32)
        return carry

    lax.fori_loop(0, BATCHES, reduce_group, 0)

    def return_sums(batch, carry):
        for k in range(1, NZD):
            line_arrival(batch, k).wait_recv()
        low_sum = jnp.zeros((8, 128), F32)
        high_sum = jnp.zeros((8, 128), F32)
        for z in range(NZD):
            part = line_in[batch, z]
            low_sum = low_sum + jnp.where(z < own_z, part, 0.0)
            high_sum = high_sum + jnp.where(z > own_z, part, 0.0)
        for q in range(NQ):
            back[batch, q, 0] = low_sum
            low_sum = low_sum + group_in[batch, q, 0]
            back[batch, NQ - 1 - q, 1] = high_sum
            high_sum = high_sum + group_in[batch, NQ - 1 - q, 1]
        for k in FAR_FIRST:
            back_copy(batch, (own_q + k) % NQ, own_q).start()
        pltpu.make_async_copy(
            back.at[batch, own_q], sums_hbm.at[batch, own_q], back_recv.at[batch, own_q]
        ).start()
        return carry

    lax.fori_loop(0, BATCHES, return_sums, 0)

    for k in range(1, NQ):
        peer = (own_q + k) % NQ
        pack_copy(peer, peer).wait_send()
    for k in range(1, NZD):
        peer = (own_z + k) % NZD
        pass_copy(peer, peer).wait_send()

    def wait_sends(i, carry):
        wait_x((STEPS - 1) % 2, i, None, "send")
        return carry

    lax.fori_loop(0, CHUNKS, wait_sends, 0)

    def wait_sums(i, carry):
        for k in range(1, NQ):
            peer = (own_q + k) % NQ
            group_copy(i, peer, peer).wait_send()
        for k in range(1, NZD):
            line_arrival(i, k).wait_send()
        return carry

    lax.fori_loop(0, BATCHES, wait_sums, 0)
    wait_y((STEPS - 1) % 2, None, "send")
    store_last.wait()
    store_image.wait()

    def finish(batch, carry):
        for k in range(1, NQ):
            peer = (own_q + k) % NQ
            back_copy(batch, peer, peer).wait()
        pltpu.make_async_copy(
            back.at[batch, own_q], sums_hbm.at[batch, own_q], back_recv.at[batch, own_q]
        ).wait()
        return carry

    lax.fori_loop(0, BATCHES, finish, 0)


def update_kernel(
    factor_ref,
    image_ref,
    sums_ref,
    last_ref,
    courant_ref,
    first_ref,
    second_ref,
    courant_out,
    first_out,
    second_out,
    last_out,
    fresh,
    store_sem,
):
    gx = lax.axis_index("gx")
    store_last = pltpu.make_async_copy(last_ref, last_out, store_sem.at[3, 0])
    store_last.start()
    rise = [factor_ref[gx * CX + x] for x in range(CX)]
    fall = [factor_ref[NG * CX + gx * CX + x] for x in range(CX)]

    def stores(part):
        band = pl.ds(part * UPDATE_ROWS, UPDATE_ROWS)
        return [
            pltpu.make_async_copy(fresh.at[k, :, band, :], out.at[:, band, :], store_sem.at[k, part])
            for k, out in enumerate((courant_out, first_out, second_out))
        ]

    for part in range(CY // UPDATE_ROWS):

        def body(j, carry):
            r = pl.ds(pl.multiple_of(part * UPDATE_ROWS + j * 8, 8), 8)
            row_tile = part * (UPDATE_ROWS // 8) + j
            turn = (CHUNKS - row_tile // (ROWS // 8)) % CHUNKS
            batch = turn // GROUP
            q = (turn % GROUP) * (NQ // GROUP) + 2 * (row_tile % (ROWS // 8))
            low, high = (
                jnp.concatenate([sums_ref[batch, q, k], sums_ref[batch, q + 1, k]], axis=1)
                for k in range(2)
            )
            values = [image_ref[x, r, :] for x in range(CX)]
            below = []
            for x in range(CX):
                low = low + rise[x] * values[x]
                below.append(low)
            for x in reversed(range(CX)):
                smoothed = fall[x] * below[x] + rise[x] * high
                high = high + fall[x] * values[x]
                first = beta_first * first_ref[x, r, :] + (1.0 - beta_first) * smoothed
                second = beta_second * second_ref[x, r, :] + (1.0 - beta_second) * smoothed * smoothed
                scaled = (1.0 / bias_second) * second
                root = scaled * lax.rsqrt(scaled)
                fresh[1, x, r, :] = first
                fresh[2, x, r, :] = second
                fresh[0, x, r, :] = courant_ref[x, r, :] - (learning_rate / bias_first) * first / (
                    root + epsilon
                )
            return carry

        lax.fori_loop(0, UPDATE_ROWS // 8, body, 0)
        for copy in stores(part):
            copy.start()
    for part in range(CY // UPDATE_ROWS):
        for copy in stores(part):
            copy.wait()
    store_last.wait()


def shards(
    courant,
    first_moment,
    second_moment,
    adjoint_prev,
    adjoint_now,
    forward_field,
    traces,
    trace_slab,
    trace_cell,
    trace_shot,
    rollback,
):
    factors = jnp.asarray(smoother_factors(NG * CX))
    table = depth_table()
    shape = jax.ShapeDtypeStruct((CX, CY, NZ), F32)
    anywhere = pl.BlockSpec(memory_space=pl.ANY)
    hbm = pl.BlockSpec(memory_space=pltpu.HBM)
    smem = pl.BlockSpec(memory_space=pltpu.SMEM)
    vmem = pl.BlockSpec(memory_space=pltpu.VMEM)
    dma = pltpu.SemaphoreType.DMA
    image, last, sums = pl.pallas_call(
        window_kernel,
        out_shape=(shape, shape, jax.ShapeDtypeStruct((BATCHES, NQ, 2, 8, 128), F32)),
        in_specs=[hbm] * 11,
        out_specs=(anywhere,) * 3,
        scratch_shapes=[
            pltpu.SMEM((SHOTS,), jnp.int32),
            pltpu.SMEM((2 * NG * CX,), F32),
            pltpu.VMEM((2, NZ, NZ), jnp.bfloat16),
            pltpu.VMEM((1, BLOCKS, 128), F32),
            pltpu.VMEM((1, BLOCKS), jnp.int32),
            pltpu.VMEM((1, BLOCKS), jnp.int32),
            pltpu.VMEM((1, BLOCKS), jnp.int32),
            pltpu.VMEM((2, CX + 8, CY + 16, NZ), F32),
            pltpu.VMEM((CX, CY, NZ), F32),
            pltpu.VMEM((STEPS, CX, CY, NZ), jnp.bfloat16),
            pltpu.VMEM((CX, CY, NZ), F32),
            pltpu.VMEM((CY, 128), F32),
            pltpu.VMEM((NQ, NZD, 1, 128), F32),
            pltpu.VMEM((NQ, NZD, 1, 128), F32),
            pltpu.VMEM((NZD, NQ, 1, 128), F32),
            pltpu.VMEM((CX, ROWS, NZ), F32),
            pltpu.VMEM((BATCHES, NQ, 2, 8, 128), F32),
            pltpu.VMEM((BATCHES, NQ, 2, 8, 128), F32),
            pltpu.VMEM((BATCHES, 2, 8, 128), F32),
            pltpu.VMEM((BATCHES, NZD, 8, 128), F32),
            pltpu.VMEM((BATCHES, NQ, 2, 8, 128), F32),
            dma((11,)),
            pltpu.SemaphoreType.REGULAR((2, 3)),
            dma((NQ,)),
            dma((NQ,)),
            dma((NZD,)),
            dma((NZD,)),
            dma((2, 2, CHUNKS)),
            dma((2, 2, CHUNKS)),
            dma((2, 2)),
            dma((2, 2)),
            dma((2, 2, CHUNKS)),
            dma((2, 2, CHUNKS)),
            dma((2, 2)),
            dma((2, 2)),
            dma((BATCHES, NQ)),
            dma((BATCHES, NQ)),
            dma((BATCHES, NZD)),
            dma((BATCHES, NZD)),
            dma((BATCHES, NQ)),
            dma((BATCHES, NQ)),
            dma((2,)),
        ],
        compiler_params=pltpu.CompilerParams(
            collective_id=0, has_side_effects=True, vmem_limit_bytes=24 << 20
        ),
    )(
        *(
            pltpu.with_memory_space_constraint(operand, pltpu.HBM)
            for operand in (
                rollback,
                factors,
                table,
                traces,
                trace_slab.reshape(1, BLOCKS),
                trace_cell,
                trace_shot,
                courant,
                adjoint_prev,
                adjoint_now,
                forward_field,
            )
        )
    )

    return pl.pallas_call(
        update_kernel,
        out_shape=(shape,) * 4,
        in_specs=[smem] + [vmem] * 6,
        out_specs=(anywhere,) * 4,
        scratch_shapes=[pltpu.VMEM((3, CX, CY, NZ), F32), dma((4, CY // UPDATE_ROWS))],
        compiler_params=pltpu.CompilerParams(vmem_limit_bytes=24 << 20),
    )(factors, image, sums, last, courant, first_moment, second_moment)


def solution(mesh):
    in_specs = (
        P("gx", "gy", None),
        P("gx", "gy", None),
        P("gx", "gy", None),
        P("gx", "gy", None),
        P("gx", "gy", None),
        P(None, "gx", "gy", None),
        P("gy", "gx", None),
        P("gy", "gx", None),
        P("gy", "gx"),
        P("gy", "gx"),
        P(),
    )
    out_specs = (P("gx", "gy", None),) * 4
    return jax.shard_map(shards, mesh=mesh, in_specs=in_specs, out_specs=out_specs, check_vma=False)
```

```python
import math

import jax
import jax.numpy as jnp
import numpy as np
from jax import lax
from jax.experimental import pallas as pl
from jax.experimental.pallas import tpu as pltpu
from jax.sharding import PartitionSpec as P

MESH = pl.DeviceIdType.MESH
F32 = jnp.float32
HIGHEST = lax.Precision.HIGHEST

STEPS = 4
SAMPLES_PER_STEP = 32
ZREC = 8
SHOTS = 16
NG = 64
NYD = 4
NQ = 8
NZD = 8
CX, CY, NZ = 8, 128, 256
BLOCKS = 128
SLOTS = 4
ROWS = 16
CHUNKS = CY // ROWS
GROUP = 32 // ROWS
BATCHES = CHUNKS // GROUP
PASS_AFTER = 3
FAR_FIRST = (4, 3, 5, 2, 6, 7, 1)
UPDATE_ROWS = 16

coefficients = (8.0 / 5.0, -1.0 / 5.0, 8.0 / 315.0, -1.0 / 560.0)
center_weight = -205.0 / 72.0
smooth_length = 4096.0
cosh_value = 1.0 + 0.5 / smooth_length
theta = math.log(cosh_value + math.sqrt(cosh_value * cosh_value - 1.0))
image_gain = 10.0
beta_first = 0.9
beta_second = 0.999
bias_first = 1.0 - 0.9**10
bias_second = 1.0 - 0.999**10
learning_rate = 0.01
epsilon = 1e-08


def depth_table():
    table = np.zeros((NZ, NZ), np.float64)
    for i in range(NZ):
        for k, w in enumerate(coefficients, 1):
            if i + k < NZ:
                table[i + k, i] = w
                table[i, i + k] = w
    table = jnp.asarray(table.astype(np.float32))
    high = table.astype(jnp.bfloat16)
    return jnp.stack([high, (table - high.astype(F32)).astype(jnp.bfloat16)])


def smoother_factors(count):
    position = np.arange(count, dtype=np.float64)
    scale = math.sqrt(image_gain / (smooth_length * math.sinh(theta) * math.sinh(theta * (count + 1))))
    rise = scale * np.sinh(theta * (position + 1.0))
    fall = scale * np.sinh(theta * (count - position))
    return np.concatenate([rise, fall]).astype(np.float32)


def iota(shape, dim):
    return lax.broadcasted_iota(jnp.int32, shape, dim)


def window_kernel(
    rollback_hbm,
    factor_hbm,
    table_hbm,
    traces_hbm,
    slab_hbm,
    cell_hbm,
    shot_hbm,
    courant_hbm,
    prev_hbm,
    now_hbm,
    forward_hbm,
    image_hbm,
    last_hbm,
    sums_hbm,
    rollback_ref,
    factor_ref,
    table_ref,
    traces_ref,
    slab_ref,
    cell_ref,
    shot_ref,
    field,
    courant,
    forward,
    image,
    source,
    packed,
    passed,
    landed,
    depth,
    plane,
    group_in,
    total,
    line_in,
    back,
    load_sem,
    known_sem,
    pack_send,
    pack_recv,
    pass_send,
    pass_recv,
    x_send,
    x_recv,
    y_send,
    y_recv,
    x_half_send,
    x_half_recv,
    y_half_send,
    y_half_recv,
    group_send,
    group_recv,
    line_send,
    line_recv,
    back_send,
    back_recv,
    store_sem,
):
    gx = lax.axis_index("gx")
    gy = lax.axis_index("gy")
    own_z = gx // NQ
    own_q = gx % NQ

    def at_group(q):
        return {"gx": own_z * NQ + q}

    def at_line(z):
        return {"gx": z * NQ + own_q}

    def remote(source_ref, target_ref, send_sem, recv_sem, device):
        return pltpu.make_async_remote_copy(
            src_ref=source_ref,
            dst_ref=target_ref,
            send_sem=send_sem,
            recv_sem=recv_sem,
            device_id=device,
            device_id_type=MESH,
        )

    def signal(sem, device):
        pl.semaphore_signal(sem, inc=1, device_id=device, device_id_type=MESH)

    barrier = pltpu.get_barrier_semaphore()
    at_edge = own_q % (NQ - 1) == 0
    for k in range(1, NQ):
        signal(barrier, at_group((own_q + k) % NQ))
    for k in (1, NYD - 1):
        signal(barrier, {"gy": (gy + k) % NYD})
    for k in (1, NZD - 1):
        signal(barrier, at_line((own_z + k) % NZD))
    across = (gx + 1 - 2 * ((NQ - 1 - own_q) // (NQ - 1)) + NG) % NG

    @pl.when(at_edge)
    def _():
        signal(barrier, {"gx": across})

    small = [
        pltpu.make_async_copy(source_ref, target_ref, load_sem.at[4 + k])
        for k, (source_ref, target_ref) in enumerate(
            (
                (traces_hbm, traces_ref),
                (slab_hbm, slab_ref),
                (cell_hbm, cell_ref),
                (shot_hbm, shot_ref),
                (rollback_hbm, rollback_ref),
                (table_hbm, table_ref),
                (factor_hbm, factor_ref),
            )
        )
    ]
    for copy in small:
        copy.start()
    loads = [
        pltpu.make_async_copy(
            now_hbm, field.at[0, pl.ds(4, CX), pl.ds(8, CY), :], load_sem.at[0]
        ),
        pltpu.make_async_copy(
            prev_hbm, field.at[1, pl.ds(4, CX), pl.ds(8, CY), :], load_sem.at[1]
        ),
        pltpu.make_async_copy(courant_hbm, courant, load_sem.at[2]),
        pltpu.make_async_copy(forward_hbm, forward, load_sem.at[3]),
    ]
    for copy in loads:
        copy.start()

    @pl.when(gx == 0)
    def _():
        field[:, 0:4, 8 : 8 + CY, :] = jnp.zeros((2, 4, CY, NZ), F32)

    @pl.when(gx == NG - 1)
    def _():
        field[:, 12:16, 8 : 8 + CY, :] = jnp.zeros((2, 4, CY, NZ), F32)

    @pl.when(gy == 0)
    def _():
        field[:, 4:12, 0:8, :] = jnp.zeros((2, CX, 8, NZ), F32)

    @pl.when(gy == NYD - 1)
    def _():
        field[:, 4:12, 8 + CY : 16 + CY, :] = jnp.zeros((2, CX, 8, NZ), F32)

    pl.semaphore_wait(barrier, NQ - 1 + 4 + 1 - (own_q % (NQ - 1) + NQ - 2) // (NQ - 1))

    has_low, has_high = gx > 0, gx < NG - 1
    y_has_low, y_has_high = gy > 0, gy < NYD - 1
    x_low = {"gx": (gx + NG - 1) % NG}
    x_high = {"gx": (gx + 1) % NG}
    y_low = {"gy": (gy + NYD - 1) % NYD}
    y_high = {"gy": (gy + 1) % NYD}
    every = pl.ds(0, NZ)

    def order(i):
        return (CHUNKS - i) % CHUNKS

    def band_of(chunk, start):
        return pl.ds(pl.multiple_of(start + chunk * ROWS, 8), ROWS)

    def x_pair(parity, chunk, sources, lanes, send, recv):
        band = band_of(chunk, 8)
        low = remote(
            sources[0], field.at[parity, pl.ds(12, 4), band, lanes], send(0), recv(1), x_low
        )
        high = remote(
            sources[1], field.at[parity, pl.ds(0, 4), band, lanes], send(1), recv(0), x_high
        )
        return low, high

    def x_field(parity, chunk, half=None):
        band = band_of(chunk, 8)
        if half is None:
            lanes = every
            send = lambda side: x_send.at[parity, side, chunk]
            recv = lambda side: x_recv.at[parity, side, chunk]
        else:
            lanes = pl.ds(half * 128, 128)
            send = lambda side: x_half_send.at[half, side, chunk]
            recv = lambda side: x_half_recv.at[half, side, chunk]
        sources = (
            field.at[parity, pl.ds(4, 4), band, lanes],
            field.at[parity, pl.ds(8, 4), band, lanes],
        )
        return x_pair(parity, chunk, sources, lanes, send, recv)

    def y_pair(parity, sources, lanes, send, recv):
        low = remote(
            sources[0],
            field.at[parity, pl.ds(4, CX), pl.ds(8 + CY, 8), lanes],
            send(0),
            recv(1),
            y_low,
        )
        high = remote(
            sources[1], field.at[parity, pl.ds(4, CX), pl.ds(0, 8), lanes], send(1), recv(0), y_high
        )
        return low, high

    def y_field(parity, half=None):
        if half is None:
            lanes = every
            send = lambda side: y_send.at[parity, side]
            recv = lambda side: y_recv.at[parity, side]
        else:
            lanes = pl.ds(half * 128, 128)
            send = lambda side: y_half_send.at[half, side]
            recv = lambda side: y_half_recv.at[half, side]
        sources = (
            field.at[parity, pl.ds(4, CX), pl.ds(8, 8), lanes],
            field.at[parity, pl.ds(4, CX), pl.ds(CY, 8), lanes],
        )
        return y_pair(parity, sources, lanes, send, recv)

    low, high = y_pair(
        0,
        (now_hbm.at[:, pl.ds(0, 8), :], now_hbm.at[:, pl.ds(CY - 8, 8), :]),
        every,
        lambda side: y_send.at[0, side],
        lambda side: y_recv.at[0, side],
    )
    pl.when(y_has_low)(low.start)
    pl.when(y_has_high)(high.start)

    def send_now(i, carry):
        chunk = order(i)
        band = band_of(chunk, 0)
        low, high = x_pair(
            0,
            chunk,
            (now_hbm.at[pl.ds(0, 4), band, :], now_hbm.at[pl.ds(4, 4), band, :]),
            every,
            lambda side: x_send.at[0, side, chunk],
            lambda side: x_recv.at[0, side, chunk],
        )
        pl.when(has_low)(low.start)
        pl.when(has_high)(high.start)
        return carry

    line_next = at_line((own_z + 1) % NZD)
    line_prev = at_line((own_z + NZD - 1) % NZD)
    signal(known_sem.at[0, 0], line_next)
    signal(known_sem.at[1, 0], line_prev)

    for copy in small[:5]:
        copy.wait()
    rows = iota((BLOCKS, 128), 0)
    lanes = iota((BLOCKS, 128), 1)
    diagonal = rows == lanes
    slab_row = slab_ref[...].astype(F32)
    shot_row = shot_ref[...]
    cell_row = cell_ref[...].astype(F32)
    live_row = jnp.zeros((1, 128), F32)
    for s in range(SHOTS):
        flag = jnp.where(rollback_ref[s] == 0, 1.0, 0.0)
        live_row = jnp.where(shot_row == s, flag, live_row)
    live_col = jnp.sum(jnp.where(diagonal, live_row, 0.0), axis=1, keepdims=True)
    cell_col = jnp.sum(jnp.where(diagonal, cell_row, 0.0), axis=1, keepdims=True)
    slab_col = jnp.sum(jnp.where(diagonal, slab_row, 0.0), axis=1, keepdims=True)
    slot_col = jnp.sum(
        jnp.where((slab_col == slab_row) & (lanes < rows), 1.0, 0.0), axis=1, keepdims=True
    )
    pick = jnp.where((lanes % 8 == rows // SAMPLES_PER_STEP) & (lanes < 8 * SLOTS), 1.0, 0.0)
    reduced = jnp.dot(traces_ref[0], pick, precision=HIGHEST, preferred_element_type=F32)
    entries = reduced * live_col + jnp.where(lanes % 8 == STEPS, cell_col, 0.0)
    entries = jnp.where(slot_col == (lanes // 8).astype(F32), entries, 0.0)
    row = iota((NG, BLOCKS), 0)
    row_slab = (row % NZD) * NQ + row // NZD
    named = jnp.where(row_slab.astype(F32) == slab_row, 1.0, 0.0)
    packed[...] = jnp.dot(
        named, entries, precision=HIGHEST, preferred_element_type=F32
    ).reshape(NQ, NZD, 1, 128)

    def pack_copy(peer, mine):
        return remote(
            packed.at[peer], passed.at[mine], pack_send.at[peer], pack_recv.at[mine], at_group(peer)
        )

    def pass_copy(peer, mine):
        return remote(
            passed.at[:, peer], landed.at[mine], pass_send.at[peer], pass_recv.at[mine], at_line(peer)
        )

    for k in FAR_FIRST:
        pack_copy((own_q + k) % NQ, own_q).start()
    lax.fori_loop(0, CHUNKS, send_now, 0)
    passed[own_q] = packed[own_q]

    pl.semaphore_wait(known_sem.at[0, 0], 1)
    signal(known_sem.at[0, 1], line_next)
    pl.semaphore_wait(known_sem.at[1, 0], 1)
    signal(known_sem.at[1, 1], line_prev)
    pl.semaphore_wait(known_sem.at[0, 1], 1)
    signal(known_sem.at[0, 2], line_next)
    pl.semaphore_wait(known_sem.at[1, 1], 1)
    pl.semaphore_wait(known_sem.at[0, 2], 1)

    def pass_on():
        for k in range(1, NQ):
            peer = (own_q + k) % NQ
            pack_copy(peer, peer).wait_recv()
        for k in FAR_FIRST:
            pass_copy((own_z + k) % NZD, own_z).start()
        landed[own_z] = passed[:, own_z]

    for copy in loads + small[5:]:
        copy.wait()

    eight = iota((8, NZ), 0)
    at_depth = iota((8, 128), 1) == ZREC
    rise = [factor_ref[gx * CX + x] for x in range(CX)]
    fall = [factor_ref[NG * CX + gx * CX + x] for x in range(CX)]

    def group_copy(chunk, peer, mine):
        return remote(
            plane.at[chunk, peer],
            group_in.at[chunk, mine],
            group_send.at[chunk, peer],
            group_recv.at[chunk, mine],
            at_group(peer),
        )

    def line_copy(chunk, k):
        peer = (own_z + k) % NZD
        return remote(
            total.at[chunk, (own_z + k) // NZD],
            line_in.at[chunk, own_z],
            line_send.at[chunk, peer],
            line_recv.at[chunk, own_z],
            at_line(peer),
        )

    def line_arrival(chunk, k):
        peer = (own_z + k) % NZD
        return remote(
            total.at[chunk, 0],
            line_in.at[chunk, peer],
            line_send.at[chunk, peer],
            line_recv.at[chunk, peer],
            at_line(peer),
        )

    def back_copy(chunk, peer, mine):
        return remote(
            back.at[chunk, peer],
            sums_hbm.at[chunk, mine],
            back_send.at[chunk, peer],
            back_recv.at[chunk, mine],
            at_group(peer),
        )

    def wait_x(parity, chunk, half, what):
        low, high = x_field(parity, chunk, half)
        if what == "recv":
            pl.when(has_low)(high.wait_recv)
            pl.when(has_high)(low.wait_recv)
        else:
            pl.when(has_low)(low.wait_send)
            pl.when(has_high)(high.wait_send)

    def wait_y(parity, half, what):
        low, high = y_field(parity, half)
        if what == "recv":
            pl.when(y_has_low)(high.wait_recv)
            pl.when(y_has_high)(low.wait_recv)
        else:
            pl.when(y_has_low)(low.wait_send)
            pl.when(y_has_high)(high.wait_send)

    def parts(parity, sent_at):
        return (0, 1) if sent_at == 0 else (None,)

    def send_halo(i, chunk, parity, half):
        low, high = x_field(parity, chunk, half)
        pl.when(has_low)(low.start)
        pl.when(has_high)(high.start)
        low, high = y_field(parity, half)

        @pl.when((i == 0) & y_has_low)
        def _():
            low.start()

        @pl.when((i == 1) & y_has_high)
        def _():
            high.start()

    def advance(t):
        now, later = t % 2, (t + 1) % 2

        def chunk_body(i, carry):
            chunk = order(i)
            for half in parts(now, t - 1):
                wait_x(now, chunk, half, "recv")
            if t >= 1:
                for half in parts(later, t - 2):
                    wait_x(later, chunk, half, "send")

            @pl.when(i == 0)
            def _():
                for half in parts(now, t - 1):
                    wait_y(now, half, "recv")
                if t >= 1:
                    for half in parts(later, t - 2):
                        wait_y(later, half, "send")

            base = pl.multiple_of(chunk * ROWS, ROWS)
            waves = field[now, 4:12, pl.ds(base + 8, ROWS), :].reshape(CX * ROWS, NZ)
            wave_high = waves.astype(jnp.bfloat16)
            wave_low = (waves - wave_high.astype(F32)).astype(jnp.bfloat16)
            depth[...] = (
                jnp.dot(wave_low, table_ref[0], preferred_element_type=F32)
                + jnp.dot(wave_high, table_ref[1], preferred_element_type=F32)
                + jnp.dot(wave_high, table_ref[0], preferred_element_type=F32)
            ).reshape(CX, ROWS, NZ)

            def row_body(j, carry):
                top = pl.multiple_of(base + j * 16, 16)
                up = [jnp.zeros((8, NZ), F32)] * 2
                down = [jnp.zeros((8, NZ), F32)] * 2
                for x in range(CX):
                    wave = forward[t, x, pl.ds(top, 16), :].astype(F32)
                    for half in range(2):
                        inner = pl.multiple_of(j * 16 + half * 8, 8)
                        row = pl.multiple_of(top + half * 8, 8)
                        r = pl.ds(pl.multiple_of(row + 8, 8), 8)
                        mid = field[now, 4 + x, r, :]
                        above = field[now, 4 + x, pl.ds(row, 8), :]
                        below = field[now, 4 + x, pl.ds(pl.multiple_of(row + 16, 8), 8), :]
                        total_sum = depth[x, pl.ds(inner, 8), :] + 3.0 * center_weight * mid
                        for k, w in enumerate(coefficients, 1):
                            paired = field[now, 4 + x + k, r, :] + field[now, 4 + x - k, r, :]
                            paired += pltpu.roll(jnp.where(eight >= k, mid, below), 8 - k, 0)
                            paired += pltpu.roll(jnp.where(eight < 8 - k, mid, above), k, 0)
                            total_sum += w * paired
                        out_rows = pl.ds(row, 8)
                        following = (
                            2.0 * mid
                            - field[later, 4 + x, r, :]
                            + courant[x, out_rows, :] * total_sum
                        )
                        if t > 0:
                            following = jnp.concatenate(
                                [
                                    following[:, :128]
                                    + jnp.where(
                                        at_depth,
                                        pltpu.roll(
                                            source[out_rows, :], (ZREC - t * CX - x) % 128, 1
                                        ),
                                        0.0,
                                    ),
                                    following[:, 128:],
                                ],
                                axis=1,
                            )
                        field[later, 4 + x, r, :] = following
                        value = wave[half * 8 : half * 8 + 8] * following
                        if t > 0:
                            value += image[x, out_rows, :]
                        image[x, out_rows, :] = value
                        if t == STEPS - 1:
                            up[half] = up[half] + rise[x] * value
                            down[half] = down[half] + fall[x] * value
                if t == STEPS - 1:
                    for half in range(2):
                        for side in range(2):
                            q = (i % GROUP) * (NQ // GROUP) + j * 4 + half * 2 + side
                            plane[i // GROUP, q, 0] = up[half][:, side * 128 : side * 128 + 128]
                            plane[i // GROUP, q, 1] = down[half][:, side * 128 : side * 128 + 128]
                return carry

            lax.fori_loop(0, ROWS // 16, row_body, 0)

            if t == 0:
                send_halo(i, chunk, later, 1)
                pl.when(i == PASS_AFTER)(pass_on)
            elif t < STEPS - 1:
                send_halo(i, chunk, later, None)
            else:
                batch = i // GROUP

                @pl.when(i % GROUP == GROUP - 1)
                def _():
                    for k in FAR_FIRST:
                        group_copy(batch, (own_q + k) % NQ, own_q).start()
                    group_in[batch, own_q] = plane[batch, own_q]

            return carry

        lax.fori_loop(0, CHUNKS, chunk_body, 0)

    advance(0)

    for k in range(1, NZD):
        peer = (own_z + k) % NZD
        pass_copy(peer, peer).wait_recv()
    arrived = landed[...].reshape(NG, 128)
    lane = iota((NG, 128), 1)
    spread = jnp.zeros((CY, 128), F32)
    for j in range(SLOTS):
        cell = arrived[:, 8 * j + STEPS : 8 * j + STEPS + 1].astype(jnp.int32)
        weights = jnp.zeros((NG, 128), F32)
        for t in range(STEPS):
            weights = jnp.where(lane // CX == t, arrived[:, 8 * j + t : 8 * j + t + 1], weights)
        weights = jnp.where(lane % CX == cell // CY, weights, 0.0)
        spot = jnp.where(lane == cell % CY, 1.0, 0.0)
        spread = spread + lax.dot_general(
            spot, weights, (((0,), (0,)), ((), ())), precision=HIGHEST, preferred_element_type=F32
        )
    source[...] = spread

    def inject(i, carry):
        chunk = order(i)
        out_rows = band_of(chunk, 0)
        in_rows = band_of(chunk, 8)
        packed_rows = source[out_rows, :]
        at_depth = iota((ROWS, 128), 1) == ZREC
        for x in range(CX):
            added = jnp.where(at_depth, pltpu.roll(packed_rows, (ZREC - x) % 128, 1), 0.0)
            wave = forward[0, x, out_rows, 0:128].astype(F32)
            field[1, 4 + x, in_rows, 0:128] += added
            image[x, out_rows, 0:128] += wave * added
        send_halo(i, chunk, 1, 0)
        return carry

    lax.fori_loop(0, CHUNKS, inject, 0)

    for t in range(1, STEPS):
        advance(t)

    store_last = pltpu.make_async_copy(
        field.at[STEPS % 2, pl.ds(4, CX), pl.ds(8, CY), :], last_hbm, store_sem.at[0]
    )
    store_image = pltpu.make_async_copy(image, image_hbm, store_sem.at[1])

    def reduce_group(batch, carry):
        for k in range(1, NQ):
            peer = (own_q + k) % NQ
            group_copy(batch, peer, peer).wait_recv()
        below_sum = group_in[batch, 0, 0]
        above_sum = group_in[batch, NQ - 1, 1]
        for q in range(1, NQ):
            below_sum = below_sum + group_in[batch, q, 0]
            above_sum = above_sum + group_in[batch, NQ - 1 - q, 1]
        total[batch, 0] = below_sum
        total[batch, 1] = above_sum
        for k in FAR_FIRST:
            line_copy(batch, k).start()
        line_in[batch, own_z] = jnp.zeros((8, 128), F32)
        return carry

    lax.fori_loop(0, BATCHES, reduce_group, 0)

    def return_sums(batch, carry):
        for k in range(1, NZD):
            line_arrival(batch, k).wait_recv()
        low_sum = jnp.zeros((8, 128), F32)
        high_sum = jnp.zeros((8, 128), F32)
        for z in range(NZD):
            part = line_in[batch, z]
            low_sum = low_sum + jnp.where(z < own_z, part, 0.0)
            high_sum = high_sum + jnp.where(z > own_z, part, 0.0)
        for q in range(NQ):
            back[batch, q, 0] = low_sum
            low_sum = low_sum + group_in[batch, q, 0]
            back[batch, NQ - 1 - q, 1] = high_sum
            high_sum = high_sum + group_in[batch, NQ - 1 - q, 1]
        for k in FAR_FIRST:
            back_copy(batch, (own_q + k) % NQ, own_q).start()
        pltpu.make_async_copy(
            back.at[batch, own_q], sums_hbm.at[batch, own_q], back_recv.at[batch, own_q]
        ).start()
        return carry

    lax.fori_loop(0, BATCHES, return_sums, 0)
    store_last.start()
    store_image.start()

    for k in range(1, NQ):
        peer = (own_q + k) % NQ
        pack_copy(peer, peer).wait_send()
    for k in range(1, NZD):
        peer = (own_z + k) % NZD
        pass_copy(peer, peer).wait_send()

    def wait_sends(i, carry):
        wait_x((STEPS - 1) % 2, i, None, "send")
        return carry

    lax.fori_loop(0, CHUNKS, wait_sends, 0)

    def wait_sums(i, carry):
        for k in range(1, NQ):
            peer = (own_q + k) % NQ
            group_copy(i, peer, peer).wait_send()
        for k in range(1, NZD):
            line_arrival(i, k).wait_send()
        return carry

    lax.fori_loop(0, BATCHES, wait_sums, 0)
    wait_y((STEPS - 1) % 2, None, "send")
    store_last.wait()
    store_image.wait()

    def finish(batch, carry):
        for k in range(1, NQ):
            peer = (own_q + k) % NQ
            back_copy(batch, peer, peer).wait()
        pltpu.make_async_copy(
            back.at[batch, own_q], sums_hbm.at[batch, own_q], back_recv.at[batch, own_q]
        ).wait()
        return carry

    lax.fori_loop(0, BATCHES, finish, 0)


def update_kernel(
    factor_ref,
    image_ref,
    sums_ref,
    last_ref,
    courant_ref,
    first_ref,
    second_ref,
    courant_out,
    first_out,
    second_out,
    last_out,
    fresh,
    store_sem,
):
    gx = lax.axis_index("gx")
    store_last = pltpu.make_async_copy(last_ref, last_out, store_sem.at[3, 0])
    store_last.start()
    rise = [factor_ref[gx * CX + x] for x in range(CX)]
    fall = [factor_ref[NG * CX + gx * CX + x] for x in range(CX)]

    def stores(part):
        band = pl.ds(part * UPDATE_ROWS, UPDATE_ROWS)
        return [
            pltpu.make_async_copy(fresh.at[k, :, band, :], out.at[:, band, :], store_sem.at[k, part])
            for k, out in enumerate((courant_out, first_out, second_out))
        ]

    for part in range(CY // UPDATE_ROWS):

        def body(j, carry):
            r = pl.ds(pl.multiple_of(part * UPDATE_ROWS + j * 8, 8), 8)
            row_tile = part * (UPDATE_ROWS // 8) + j
            turn = (CHUNKS - row_tile // (ROWS // 8)) % CHUNKS
            batch = turn // GROUP
            q = (turn % GROUP) * (NQ // GROUP) + 2 * (row_tile % (ROWS // 8))
            low, high = (
                jnp.concatenate([sums_ref[batch, q, k], sums_ref[batch, q + 1, k]], axis=1)
                for k in range(2)
            )
            values = [image_ref[x, r, :] for x in range(CX)]
            below = []
            for x in range(CX):
                low = low + rise[x] * values[x]
                below.append(low)
            for x in reversed(range(CX)):
                smoothed = fall[x] * below[x] + rise[x] * high
                high = high + fall[x] * values[x]
                first = beta_first * first_ref[x, r, :] + (1.0 - beta_first) * smoothed
                second = beta_second * second_ref[x, r, :] + (1.0 - beta_second) * smoothed * smoothed
                scaled = (1.0 / bias_second) * second
                root = scaled * lax.rsqrt(scaled)
                fresh[1, x, r, :] = first
                fresh[2, x, r, :] = second
                fresh[0, x, r, :] = courant_ref[x, r, :] - (learning_rate / bias_first) * first / (
                    root + epsilon
                )
            return carry

        lax.fori_loop(0, UPDATE_ROWS // 8, body, 0)
        for copy in stores(part):
            copy.start()
    for part in range(CY // UPDATE_ROWS):
        for copy in stores(part):
            copy.wait()
    store_last.wait()


def shards(
    courant,
    first_moment,
    second_moment,
    adjoint_prev,
    adjoint_now,
    forward_field,
    traces,
    trace_slab,
    trace_cell,
    trace_shot,
    rollback,
):
    factors = jnp.asarray(smoother_factors(NG * CX))
    table = depth_table()
    shape = jax.ShapeDtypeStruct((CX, CY, NZ), F32)
    anywhere = pl.BlockSpec(memory_space=pl.ANY)
    hbm = pl.BlockSpec(memory_space=pltpu.HBM)
    smem = pl.BlockSpec(memory_space=pltpu.SMEM)
    vmem = pl.BlockSpec(memory_space=pltpu.VMEM)
    dma = pltpu.SemaphoreType.DMA
    image, last, sums = pl.pallas_call(
        window_kernel,
        out_shape=(shape, shape, jax.ShapeDtypeStruct((BATCHES, NQ, 2, 8, 128), F32)),
        in_specs=[hbm] * 11,
        out_specs=(anywhere,) * 3,
        scratch_shapes=[
            pltpu.SMEM((SHOTS,), jnp.int32),
            pltpu.SMEM((2 * NG * CX,), F32),
            pltpu.VMEM((2, NZ, NZ), jnp.bfloat16),
            pltpu.VMEM((1, BLOCKS, 128), F32),
            pltpu.VMEM((1, BLOCKS), jnp.int32),
            pltpu.VMEM((1, BLOCKS), jnp.int32),
            pltpu.VMEM((1, BLOCKS), jnp.int32),
            pltpu.VMEM((2, CX + 8, CY + 16, NZ), F32),
            pltpu.VMEM((CX, CY, NZ), F32),
            pltpu.VMEM((STEPS, CX, CY, NZ), jnp.bfloat16),
            pltpu.VMEM((CX, CY, NZ), F32),
            pltpu.VMEM((CY, 128), F32),
            pltpu.VMEM((NQ, NZD, 1, 128), F32),
            pltpu.VMEM((NQ, NZD, 1, 128), F32),
            pltpu.VMEM((NZD, NQ, 1, 128), F32),
            pltpu.VMEM((CX, ROWS, NZ), F32),
            pltpu.VMEM((BATCHES, NQ, 2, 8, 128), F32),
            pltpu.VMEM((BATCHES, NQ, 2, 8, 128), F32),
            pltpu.VMEM((BATCHES, 2, 8, 128), F32),
            pltpu.VMEM((BATCHES, NZD, 8, 128), F32),
            pltpu.VMEM((BATCHES, NQ, 2, 8, 128), F32),
            dma((11,)),
            pltpu.SemaphoreType.REGULAR((2, 3)),
            dma((NQ,)),
            dma((NQ,)),
            dma((NZD,)),
            dma((NZD,)),
            dma((2, 2, CHUNKS)),
            dma((2, 2, CHUNKS)),
            dma((2, 2)),
            dma((2, 2)),
            dma((2, 2, CHUNKS)),
            dma((2, 2, CHUNKS)),
            dma((2, 2)),
            dma((2, 2)),
            dma((BATCHES, NQ)),
            dma((BATCHES, NQ)),
            dma((BATCHES, NZD)),
            dma((BATCHES, NZD)),
            dma((BATCHES, NQ)),
            dma((BATCHES, NQ)),
            dma((2,)),
        ],
        compiler_params=pltpu.CompilerParams(
            collective_id=0, has_side_effects=True, vmem_limit_bytes=24 << 20
        ),
    )(
        *(
            pltpu.with_memory_space_constraint(operand, pltpu.HBM)
            for operand in (
                rollback,
                factors,
                table,
                traces,
                trace_slab.reshape(1, BLOCKS),
                trace_cell,
                trace_shot,
                courant,
                adjoint_prev,
                adjoint_now,
                forward_field,
            )
        )
    )

    return pl.pallas_call(
        update_kernel,
        out_shape=(shape,) * 4,
        in_specs=[smem] + [vmem] * 6,
        out_specs=(anywhere,) * 4,
        scratch_shapes=[pltpu.VMEM((3, CX, CY, NZ), F32), dma((4, CY // UPDATE_ROWS))],
        compiler_params=pltpu.CompilerParams(vmem_limit_bytes=24 << 20),
    )(factors, image, sums, last, courant, first_moment, second_moment)


def solution(mesh):
    in_specs = (
        P("gx", "gy", None),
        P("gx", "gy", None),
        P("gx", "gy", None),
        P("gx", "gy", None),
        P("gx", "gy", None),
        P(None, "gx", "gy", None),
        P("gy", "gx", None),
        P("gy", "gx", None),
        P("gy", "gx"),
        P("gy", "gx"),
        P(),
    )
    out_specs = (P("gx", "gy", None),) * 4
    return jax.shard_map(shards, mesh=mesh, in_specs=in_specs, out_specs=out_specs, check_vma=False)
```

```python
import math

import jax
import jax.numpy as jnp
import numpy as np
from jax import lax
from jax.experimental import pallas as pl
from jax.experimental.pallas import tpu as pltpu
from jax.sharding import PartitionSpec as P

MESH = pl.DeviceIdType.MESH
F32 = jnp.float32
HIGHEST = lax.Precision.HIGHEST

STEPS = 4
SAMPLES_PER_STEP = 32
ZREC = 8
SHOTS = 16
NG = 64
NYD = 4
NQ = 8
NZD = 8
CX, CY, NZ = 8, 128, 256
BLOCKS = 128
SLOTS = 4
ROWS = 16
CHUNKS = CY // ROWS
GROUP = 32 // ROWS
BATCHES = CHUNKS // GROUP
PASS_AFTER = 3
FAR_FIRST = (4, 3, 5, 2, 6, 7, 1)
UPDATE_ROWS = 16

coefficients = (8.0 / 5.0, -1.0 / 5.0, 8.0 / 315.0, -1.0 / 560.0)
center_weight = -205.0 / 72.0
smooth_length = 4096.0
cosh_value = 1.0 + 0.5 / smooth_length
theta = math.log(cosh_value + math.sqrt(cosh_value * cosh_value - 1.0))
image_gain = 10.0
beta_first = 0.9
beta_second = 0.999
bias_first = 1.0 - 0.9**10
bias_second = 1.0 - 0.999**10
learning_rate = 0.01
epsilon = 1e-08


def depth_table():
    table = np.zeros((NZ, NZ), np.float64)
    for i in range(NZ):
        for k, w in enumerate(coefficients, 1):
            if i + k < NZ:
                table[i + k, i] = w
                table[i, i + k] = w
    table = jnp.asarray(table.astype(np.float32))
    high = table.astype(jnp.bfloat16)
    return jnp.stack([high, (table - high.astype(F32)).astype(jnp.bfloat16)])


def smoother_factors(count):
    position = np.arange(count, dtype=np.float64)
    scale = math.sqrt(image_gain / (smooth_length * math.sinh(theta) * math.sinh(theta * (count + 1))))
    rise = scale * np.sinh(theta * (position + 1.0))
    fall = scale * np.sinh(theta * (count - position))
    return np.concatenate([rise, fall]).astype(np.float32)


def iota(shape, dim):
    return lax.broadcasted_iota(jnp.int32, shape, dim)


def window_kernel(
    rollback_hbm,
    factor_hbm,
    table_hbm,
    traces_hbm,
    slab_hbm,
    cell_hbm,
    shot_hbm,
    courant_hbm,
    prev_hbm,
    now_hbm,
    forward_hbm,
    image_hbm,
    last_hbm,
    sums_hbm,
    rollback_ref,
    factor_ref,
    table_ref,
    traces_ref,
    slab_ref,
    cell_ref,
    shot_ref,
    field,
    courant,
    forward,
    image,
    source,
    packed,
    passed,
    landed,
    depth,
    plane,
    group_in,
    total,
    line_in,
    back,
    load_sem,
    known_sem,
    pack_send,
    pack_recv,
    pass_send,
    pass_recv,
    x_send,
    x_recv,
    y_send,
    y_recv,
    x_half_send,
    x_half_recv,
    y_half_send,
    y_half_recv,
    group_send,
    group_recv,
    line_send,
    line_recv,
    back_send,
    back_recv,
    store_sem,
):
    gx = lax.axis_index("gx")
    gy = lax.axis_index("gy")
    own_z = gx // NQ
    own_q = gx % NQ

    def at_group(q):
        return {"gx": own_z * NQ + q}

    def at_line(z):
        return {"gx": z * NQ + own_q}

    def remote(source_ref, target_ref, send_sem, recv_sem, device):
        return pltpu.make_async_remote_copy(
            src_ref=source_ref,
            dst_ref=target_ref,
            send_sem=send_sem,
            recv_sem=recv_sem,
            device_id=device,
            device_id_type=MESH,
        )

    def signal(sem, device):
        pl.semaphore_signal(sem, inc=1, device_id=device, device_id_type=MESH)

    barrier = pltpu.get_barrier_semaphore()
    at_edge = own_q % (NQ - 1) == 0
    for k in range(1, NQ):
        signal(barrier, at_group((own_q + k) % NQ))
    for k in (1, NYD - 1):
        signal(barrier, {"gy": (gy + k) % NYD})
    for k in (1, NZD - 1):
        signal(barrier, at_line((own_z + k) % NZD))
    across = (gx + 1 - 2 * ((NQ - 1 - own_q) // (NQ - 1)) + NG) % NG

    @pl.when(at_edge)
    def _():
        signal(barrier, {"gx": across})

    small = [
        pltpu.make_async_copy(source_ref, target_ref, load_sem.at[4 + k])
        for k, (source_ref, target_ref) in enumerate(
            (
                (traces_hbm, traces_ref),
                (slab_hbm, slab_ref),
                (cell_hbm, cell_ref),
                (shot_hbm, shot_ref),
                (rollback_hbm, rollback_ref),
                (table_hbm, table_ref),
                (factor_hbm, factor_ref),
            )
        )
    ]
    for copy in small:
        copy.start()
    loads = [
        pltpu.make_async_copy(
            now_hbm, field.at[0, pl.ds(4, CX), pl.ds(8, CY), :], load_sem.at[0]
        ),
        pltpu.make_async_copy(
            prev_hbm, field.at[1, pl.ds(4, CX), pl.ds(8, CY), :], load_sem.at[1]
        ),
        pltpu.make_async_copy(courant_hbm, courant, load_sem.at[2]),
        pltpu.make_async_copy(forward_hbm, forward, load_sem.at[3]),
    ]
    for copy in loads:
        copy.start()

    @pl.when(gx == 0)
    def _():
        field[:, 0:4, 8 : 8 + CY, :] = jnp.zeros((2, 4, CY, NZ), F32)

    @pl.when(gx == NG - 1)
    def _():
        field[:, 12:16, 8 : 8 + CY, :] = jnp.zeros((2, 4, CY, NZ), F32)

    @pl.when(gy == 0)
    def _():
        field[:, 4:12, 0:8, :] = jnp.zeros((2, CX, 8, NZ), F32)

    @pl.when(gy == NYD - 1)
    def _():
        field[:, 4:12, 8 + CY : 16 + CY, :] = jnp.zeros((2, CX, 8, NZ), F32)

    for copy in small[:5]:
        copy.wait()
    rows = iota((BLOCKS, 128), 0)
    lanes = iota((BLOCKS, 128), 1)
    diagonal = rows == lanes
    slab_row = slab_ref[...].astype(F32)
    shot_row = shot_ref[...]
    cell_row = cell_ref[...].astype(F32)
    live_row = jnp.zeros((1, 128), F32)
    for s in range(SHOTS):
        flag = jnp.where(rollback_ref[s] == 0, 1.0, 0.0)
        live_row = jnp.where(shot_row == s, flag, live_row)
    live_col = jnp.sum(jnp.where(diagonal, live_row, 0.0), axis=1, keepdims=True)
    cell_col = jnp.sum(jnp.where(diagonal, cell_row, 0.0), axis=1, keepdims=True)
    slab_col = jnp.sum(jnp.where(diagonal, slab_row, 0.0), axis=1, keepdims=True)
    slot_col = jnp.sum(
        jnp.where((slab_col == slab_row) & (lanes < rows), 1.0, 0.0), axis=1, keepdims=True
    )
    pick = jnp.where((lanes % 8 == rows // SAMPLES_PER_STEP) & (lanes < 8 * SLOTS), 1.0, 0.0)
    reduced = jnp.dot(traces_ref[0], pick, precision=HIGHEST, preferred_element_type=F32)
    entries = reduced * live_col + jnp.where(lanes % 8 == STEPS, cell_col, 0.0)
    entries = jnp.where(slot_col == (lanes // 8).astype(F32), entries, 0.0)
    row = iota((NG, BLOCKS), 0)
    row_slab = (row % NZD) * NQ + row // NZD
    named = jnp.where(row_slab.astype(F32) == slab_row, 1.0, 0.0)
    packed[...] = jnp.dot(
        named, entries, precision=HIGHEST, preferred_element_type=F32
    ).reshape(NQ, NZD, 1, 128)

    pl.semaphore_wait(barrier, NQ - 1 + 4 + 1 - (own_q % (NQ - 1) + NQ - 2) // (NQ - 1))

    has_low, has_high = gx > 0, gx < NG - 1
    y_has_low, y_has_high = gy > 0, gy < NYD - 1
    x_low = {"gx": (gx + NG - 1) % NG}
    x_high = {"gx": (gx + 1) % NG}
    y_low = {"gy": (gy + NYD - 1) % NYD}
    y_high = {"gy": (gy + 1) % NYD}
    every = pl.ds(0, NZ)

    def order(i):
        return (CHUNKS - i) % CHUNKS

    def band_of(chunk, start):
        return pl.ds(pl.multiple_of(start + chunk * ROWS, 8), ROWS)

    def x_pair(parity, chunk, sources, lanes, send, recv):
        band = band_of(chunk, 8)
        low = remote(
            sources[0], field.at[parity, pl.ds(12, 4), band, lanes], send(0), recv(1), x_low
        )
        high = remote(
            sources[1], field.at[parity, pl.ds(0, 4), band, lanes], send(1), recv(0), x_high
        )
        return low, high

    def x_field(parity, chunk, half=None):
        band = band_of(chunk, 8)
        if half is None:
            lanes = every
            send = lambda side: x_send.at[parity, side, chunk]
            recv = lambda side: x_recv.at[parity, side, chunk]
        else:
            lanes = pl.ds(half * 128, 128)
            send = lambda side: x_half_send.at[half, side, chunk]
            recv = lambda side: x_half_recv.at[half, side, chunk]
        sources = (
            field.at[parity, pl.ds(4, 4), band, lanes],
            field.at[parity, pl.ds(8, 4), band, lanes],
        )
        return x_pair(parity, chunk, sources, lanes, send, recv)

    def y_pair(parity, sources, lanes, send, recv):
        low = remote(
            sources[0],
            field.at[parity, pl.ds(4, CX), pl.ds(8 + CY, 8), lanes],
            send(0),
            recv(1),
            y_low,
        )
        high = remote(
            sources[1], field.at[parity, pl.ds(4, CX), pl.ds(0, 8), lanes], send(1), recv(0), y_high
        )
        return low, high

    def y_field(parity, half=None):
        if half is None:
            lanes = every
            send = lambda side: y_send.at[parity, side]
            recv = lambda side: y_recv.at[parity, side]
        else:
            lanes = pl.ds(half * 128, 128)
            send = lambda side: y_half_send.at[half, side]
            recv = lambda side: y_half_recv.at[half, side]
        sources = (
            field.at[parity, pl.ds(4, CX), pl.ds(8, 8), lanes],
            field.at[parity, pl.ds(4, CX), pl.ds(CY, 8), lanes],
        )
        return y_pair(parity, sources, lanes, send, recv)

    low, high = y_pair(
        0,
        (now_hbm.at[:, pl.ds(0, 8), :], now_hbm.at[:, pl.ds(CY - 8, 8), :]),
        every,
        lambda side: y_send.at[0, side],
        lambda side: y_recv.at[0, side],
    )
    pl.when(y_has_low)(low.start)
    pl.when(y_has_high)(high.start)

    def send_now(i, carry):
        chunk = order(i)
        band = band_of(chunk, 0)
        low, high = x_pair(
            0,
            chunk,
            (now_hbm.at[pl.ds(0, 4), band, :], now_hbm.at[pl.ds(4, 4), band, :]),
            every,
            lambda side: x_send.at[0, side, chunk],
            lambda side: x_recv.at[0, side, chunk],
        )
        pl.when(has_low)(low.start)
        pl.when(has_high)(high.start)
        return carry

    line_next = at_line((own_z + 1) % NZD)
    line_prev = at_line((own_z + NZD - 1) % NZD)
    signal(known_sem.at[0, 0], line_next)
    signal(known_sem.at[1, 0], line_prev)

    def pack_copy(peer, mine):
        return remote(
            packed.at[peer], passed.at[mine], pack_send.at[peer], pack_recv.at[mine], at_group(peer)
        )

    def pass_copy(peer, mine):
        return remote(
            passed.at[:, peer], landed.at[mine], pass_send.at[peer], pass_recv.at[mine], at_line(peer)
        )

    for k in FAR_FIRST:
        pack_copy((own_q + k) % NQ, own_q).start()
    lax.fori_loop(0, CHUNKS, send_now, 0)
    passed[own_q] = packed[own_q]

    pl.semaphore_wait(known_sem.at[0, 0], 1)
    signal(known_sem.at[0, 1], line_next)
    pl.semaphore_wait(known_sem.at[1, 0], 1)
    signal(known_sem.at[1, 1], line_prev)
    pl.semaphore_wait(known_sem.at[0, 1], 1)
    signal(known_sem.at[0, 2], line_next)
    pl.semaphore_wait(known_sem.at[1, 1], 1)
    pl.semaphore_wait(known_sem.at[0, 2], 1)

    def pass_on():
        for k in range(1, NQ):
            peer = (own_q + k) % NQ
            pack_copy(peer, peer).wait_recv()
        for k in FAR_FIRST:
            pass_copy((own_z + k) % NZD, own_z).start()
        landed[own_z] = passed[:, own_z]

    for copy in loads + small[5:]:
        copy.wait()

    eight = iota((8, NZ), 0)
    at_depth = iota((8, 128), 1) == ZREC
    rise = [factor_ref[gx * CX + x] for x in range(CX)]
    fall = [factor_ref[NG * CX + gx * CX + x] for x in range(CX)]

    def group_copy(chunk, peer, mine):
        return remote(
            plane.at[chunk, peer],
            group_in.at[chunk, mine],
            group_send.at[chunk, peer],
            group_recv.at[chunk, mine],
            at_group(peer),
        )

    def line_copy(chunk, k):
        peer = (own_z + k) % NZD
        return remote(
            total.at[chunk, (own_z + k) // NZD],
            line_in.at[chunk, own_z],
            line_send.at[chunk, peer],
            line_recv.at[chunk, own_z],
            at_line(peer),
        )

    def line_arrival(chunk, k):
        peer = (own_z + k) % NZD
        return remote(
            total.at[chunk, 0],
            line_in.at[chunk, peer],
            line_send.at[chunk, peer],
            line_recv.at[chunk, peer],
            at_line(peer),
        )

    def back_copy(chunk, peer, mine):
        return remote(
            back.at[chunk, peer],
            sums_hbm.at[chunk, mine],
            back_send.at[chunk, peer],
            back_recv.at[chunk, mine],
            at_group(peer),
        )

    def wait_x(parity, chunk, half, what):
        low, high = x_field(parity, chunk, half)
        if what == "recv":
            pl.when(has_low)(high.wait_recv)
            pl.when(has_high)(low.wait_recv)
        else:
            pl.when(has_low)(low.wait_send)
            pl.when(has_high)(high.wait_send)

    def wait_y(parity, half, what):
        low, high = y_field(parity, half)
        if what == "recv":
            pl.when(y_has_low)(high.wait_recv)
            pl.when(y_has_high)(low.wait_recv)
        else:
            pl.when(y_has_low)(low.wait_send)
            pl.when(y_has_high)(high.wait_send)

    def parts(parity, sent_at):
        return (0, 1) if sent_at == 0 else (None,)

    def send_halo(i, chunk, parity, half):
        low, high = x_field(parity, chunk, half)
        pl.when(has_low)(low.start)
        pl.when(has_high)(high.start)
        low, high = y_field(parity, half)

        @pl.when((i == 0) & y_has_low)
        def _():
            low.start()

        @pl.when((i == 1) & y_has_high)
        def _():
            high.start()

    def advance(t):
        now, later = t % 2, (t + 1) % 2

        def chunk_body(i, carry):
            chunk = order(i)
            for half in parts(now, t - 1):
                wait_x(now, chunk, half, "recv")
            if t >= 1:
                for half in parts(later, t - 2):
                    wait_x(later, chunk, half, "send")

            @pl.when(i == 0)
            def _():
                for half in parts(now, t - 1):
                    wait_y(now, half, "recv")
                if t >= 1:
                    for half in parts(later, t - 2):
                        wait_y(later, half, "send")

            base = pl.multiple_of(chunk * ROWS, ROWS)
            waves = field[now, 4:12, pl.ds(base + 8, ROWS), :].reshape(CX * ROWS, NZ)
            wave_high = waves.astype(jnp.bfloat16)
            wave_low = (waves - wave_high.astype(F32)).astype(jnp.bfloat16)
            depth[...] = (
                jnp.dot(wave_low, table_ref[0], preferred_element_type=F32)
                + jnp.dot(wave_high, table_ref[1], preferred_element_type=F32)
                + jnp.dot(wave_high, table_ref[0], preferred_element_type=F32)
            ).reshape(CX, ROWS, NZ)

            def row_body(j, carry):
                top = pl.multiple_of(base + j * 16, 16)
                up = [jnp.zeros((8, NZ), F32)] * 2
                down = [jnp.zeros((8, NZ), F32)] * 2
                for x in range(CX):
                    wave = forward[t, x, pl.ds(top, 16), :].astype(F32)
                    for half in range(2):
                        inner = pl.multiple_of(j * 16 + half * 8, 8)
                        row = pl.multiple_of(top + half * 8, 8)
                        r = pl.ds(pl.multiple_of(row + 8, 8), 8)
                        mid = field[now, 4 + x, r, :]
                        above = field[now, 4 + x, pl.ds(row, 8), :]
                        below = field[now, 4 + x, pl.ds(pl.multiple_of(row + 16, 8), 8), :]
                        total_sum = depth[x, pl.ds(inner, 8), :] + 3.0 * center_weight * mid
                        for k, w in enumerate(coefficients, 1):
                            paired = field[now, 4 + x + k, r, :] + field[now, 4 + x - k, r, :]
                            paired += pltpu.roll(jnp.where(eight >= k, mid, below), 8 - k, 0)
                            paired += pltpu.roll(jnp.where(eight < 8 - k, mid, above), k, 0)
                            total_sum += w * paired
                        out_rows = pl.ds(row, 8)
                        following = (
                            2.0 * mid
                            - field[later, 4 + x, r, :]
                            + courant[x, out_rows, :] * total_sum
                        )
                        if t > 0:
                            following = jnp.concatenate(
                                [
                                    following[:, :128]
                                    + jnp.where(
                                        at_depth,
                                        pltpu.roll(
                                            source[out_rows, :], (ZREC - t * CX - x) % 128, 1
                                        ),
                                        0.0,
                                    ),
                                    following[:, 128:],
                                ],
                                axis=1,
                            )
                        field[later, 4 + x, r, :] = following
                        value = wave[half * 8 : half * 8 + 8] * following
                        if t > 0:
                            value += image[x, out_rows, :]
                        image[x, out_rows, :] = value
                        if t == STEPS - 1:
                            up[half] = up[half] + rise[x] * value
                            down[half] = down[half] + fall[x] * value
                if t == STEPS - 1:
                    for half in range(2):
                        for side in range(2):
                            q = (i % GROUP) * (NQ // GROUP) + j * 4 + half * 2 + side
                            plane[i // GROUP, q, 0] = up[half][:, side * 128 : side * 128 + 128]
                            plane[i // GROUP, q, 1] = down[half][:, side * 128 : side * 128 + 128]
                return carry

            lax.fori_loop(0, ROWS // 16, row_body, 0)

            if t == 0:
                send_halo(i, chunk, later, 1)
                pl.when(i == PASS_AFTER)(pass_on)
            elif t < STEPS - 1:
                send_halo(i, chunk, later, None)
            else:
                batch = i // GROUP

                @pl.when(i % GROUP == GROUP - 1)
                def _():
                    for k in FAR_FIRST:
                        group_copy(batch, (own_q + k) % NQ, own_q).start()
                    group_in[batch, own_q] = plane[batch, own_q]

            return carry

        lax.fori_loop(0, CHUNKS, chunk_body, 0)

    advance(0)

    for k in range(1, NZD):
        peer = (own_z + k) % NZD
        pass_copy(peer, peer).wait_recv()
    arrived = landed[...].reshape(NG, 128)
    lane = iota((NG, 128), 1)
    spread = jnp.zeros((CY, 128), F32)
    for j in range(SLOTS):
        cell = arrived[:, 8 * j + STEPS : 8 * j + STEPS + 1].astype(jnp.int32)
        weights = jnp.zeros((NG, 128), F32)
        for t in range(STEPS):
            weights = jnp.where(lane // CX == t, arrived[:, 8 * j + t : 8 * j + t + 1], weights)
        weights = jnp.where(lane % CX == cell // CY, weights, 0.0)
        spot = jnp.where(lane == cell % CY, 1.0, 0.0)
        spread = spread + lax.dot_general(
            spot, weights, (((0,), (0,)), ((), ())), precision=HIGHEST, preferred_element_type=F32
        )
    source[...] = spread

    def inject(i, carry):
        chunk = order(i)
        out_rows = band_of(chunk, 0)
        in_rows = band_of(chunk, 8)
        packed_rows = source[out_rows, :]
        at_depth = iota((ROWS, 128), 1) == ZREC
        for x in range(CX):
            added = jnp.where(at_depth, pltpu.roll(packed_rows, (ZREC - x) % 128, 1), 0.0)
            wave = forward[0, x, out_rows, 0:128].astype(F32)
            field[1, 4 + x, in_rows, 0:128] += added
            image[x, out_rows, 0:128] += wave * added
        send_halo(i, chunk, 1, 0)
        return carry

    lax.fori_loop(0, CHUNKS, inject, 0)

    for t in range(1, STEPS):
        advance(t)

    store_last = pltpu.make_async_copy(
        field.at[STEPS % 2, pl.ds(4, CX), pl.ds(8, CY), :], last_hbm, store_sem.at[0]
    )
    store_image = pltpu.make_async_copy(image, image_hbm, store_sem.at[1])

    def reduce_group(batch, carry):
        for k in range(1, NQ):
            peer = (own_q + k) % NQ
            group_copy(batch, peer, peer).wait_recv()
        below_sum = group_in[batch, 0, 0]
        above_sum = group_in[batch, NQ - 1, 1]
        for q in range(1, NQ):
            below_sum = below_sum + group_in[batch, q, 0]
            above_sum = above_sum + group_in[batch, NQ - 1 - q, 1]
        total[batch, 0] = below_sum
        total[batch, 1] = above_sum
        for k in FAR_FIRST:
            line_copy(batch, k).start()
        line_in[batch, own_z] = jnp.zeros((8, 128), F32)
        return carry

    lax.fori_loop(0, BATCHES, reduce_group, 0)

    def return_sums(batch, carry):
        for k in range(1, NZD):
            line_arrival(batch, k).wait_recv()
        low_sum = jnp.zeros((8, 128), F32)
        high_sum = jnp.zeros((8, 128), F32)
        for z in range(NZD):
            part = line_in[batch, z]
            low_sum = low_sum + jnp.where(z < own_z, part, 0.0)
            high_sum = high_sum + jnp.where(z > own_z, part, 0.0)
        for q in range(NQ):
            back[batch, q, 0] = low_sum
            low_sum = low_sum + group_in[batch, q, 0]
            back[batch, NQ - 1 - q, 1] = high_sum
            high_sum = high_sum + group_in[batch, NQ - 1 - q, 1]
        for k in FAR_FIRST:
            back_copy(batch, (own_q + k) % NQ, own_q).start()
        pltpu.make_async_copy(
            back.at[batch, own_q], sums_hbm.at[batch, own_q], back_recv.at[batch, own_q]
        ).start()
        return carry

    lax.fori_loop(0, BATCHES, return_sums, 0)
    store_last.start()
    store_image.start()

    for k in range(1, NQ):
        peer = (own_q + k) % NQ
        pack_copy(peer, peer).wait_send()
    for k in range(1, NZD):
        peer = (own_z + k) % NZD
        pass_copy(peer, peer).wait_send()

    def wait_sends(i, carry):
        wait_x((STEPS - 1) % 2, i, None, "send")
        return carry

    lax.fori_loop(0, CHUNKS, wait_sends, 0)

    def wait_sums(i, carry):
        for k in range(1, NQ):
            peer = (own_q + k) % NQ
            group_copy(i, peer, peer).wait_send()
        for k in range(1, NZD):
            line_arrival(i, k).wait_send()
        return carry

    lax.fori_loop(0, BATCHES, wait_sums, 0)
    wait_y((STEPS - 1) % 2, None, "send")
    store_last.wait()
    store_image.wait()

    def finish(batch, carry):
        for k in range(1, NQ):
            peer = (own_q + k) % NQ
            back_copy(batch, peer, peer).wait()
        pltpu.make_async_copy(
            back.at[batch, own_q], sums_hbm.at[batch, own_q], back_recv.at[batch, own_q]
        ).wait()
        return carry

    lax.fori_loop(0, BATCHES, finish, 0)


def update_kernel(
    factor_ref,
    image_ref,
    sums_ref,
    last_ref,
    courant_ref,
    first_ref,
    second_ref,
    courant_out,
    first_out,
    second_out,
    last_out,
    fresh,
    store_sem,
):
    gx = lax.axis_index("gx")
    store_last = pltpu.make_async_copy(last_ref, last_out, store_sem.at[3, 0])
    store_last.start()
    rise = [factor_ref[gx * CX + x] for x in range(CX)]
    fall = [factor_ref[NG * CX + gx * CX + x] for x in range(CX)]

    def stores(part):
        band = pl.ds(part * UPDATE_ROWS, UPDATE_ROWS)
        return [
            pltpu.make_async_copy(fresh.at[k, :, band, :], out.at[:, band, :], store_sem.at[k, part])
            for k, out in enumerate((courant_out, first_out, second_out))
        ]

    for part in range(CY // UPDATE_ROWS):

        def body(j, carry):
            r = pl.ds(pl.multiple_of(part * UPDATE_ROWS + j * 8, 8), 8)
            row_tile = part * (UPDATE_ROWS // 8) + j
            turn = (CHUNKS - row_tile // (ROWS // 8)) % CHUNKS
            batch = turn // GROUP
            q = (turn % GROUP) * (NQ // GROUP) + 2 * (row_tile % (ROWS // 8))
            low, high = (
                jnp.concatenate([sums_ref[batch, q, k], sums_ref[batch, q + 1, k]], axis=1)
                for k in range(2)
            )
            values = [image_ref[x, r, :] for x in range(CX)]
            below = []
            for x in range(CX):
                low = low + rise[x] * values[x]
                below.append(low)
            for x in reversed(range(CX)):
                smoothed = fall[x] * below[x] + rise[x] * high
                high = high + fall[x] * values[x]
                first = beta_first * first_ref[x, r, :] + (1.0 - beta_first) * smoothed
                second = beta_second * second_ref[x, r, :] + (1.0 - beta_second) * smoothed * smoothed
                scaled = (1.0 / bias_second) * second
                root = scaled * lax.rsqrt(scaled)
                fresh[1, x, r, :] = first
                fresh[2, x, r, :] = second
                fresh[0, x, r, :] = courant_ref[x, r, :] - (learning_rate / bias_first) * first / (
                    root + epsilon
                )
            return carry

        lax.fori_loop(0, UPDATE_ROWS // 8, body, 0)
        for copy in stores(part):
            copy.start()
    for part in range(CY // UPDATE_ROWS):
        for copy in stores(part):
            copy.wait()
    store_last.wait()


def shards(
    courant,
    first_moment,
    second_moment,
    adjoint_prev,
    adjoint_now,
    forward_field,
    traces,
    trace_slab,
    trace_cell,
    trace_shot,
    rollback,
):
    factors = jnp.asarray(smoother_factors(NG * CX))
    table = depth_table()
    shape = jax.ShapeDtypeStruct((CX, CY, NZ), F32)
    anywhere = pl.BlockSpec(memory_space=pl.ANY)
    hbm = pl.BlockSpec(memory_space=pltpu.HBM)
    smem = pl.BlockSpec(memory_space=pltpu.SMEM)
    vmem = pl.BlockSpec(memory_space=pltpu.VMEM)
    dma = pltpu.SemaphoreType.DMA
    image, last, sums = pl.pallas_call(
        window_kernel,
        out_shape=(shape, shape, jax.ShapeDtypeStruct((BATCHES, NQ, 2, 8, 128), F32)),
        in_specs=[hbm] * 11,
        out_specs=(anywhere,) * 3,
        scratch_shapes=[
            pltpu.SMEM((SHOTS,), jnp.int32),
            pltpu.SMEM((2 * NG * CX,), F32),
            pltpu.VMEM((2, NZ, NZ), jnp.bfloat16),
            pltpu.VMEM((1, BLOCKS, 128), F32),
            pltpu.VMEM((1, BLOCKS), jnp.int32),
            pltpu.VMEM((1, BLOCKS), jnp.int32),
            pltpu.VMEM((1, BLOCKS), jnp.int32),
            pltpu.VMEM((2, CX + 8, CY + 16, NZ), F32),
            pltpu.VMEM((CX, CY, NZ), F32),
            pltpu.VMEM((STEPS, CX, CY, NZ), jnp.bfloat16),
            pltpu.VMEM((CX, CY, NZ), F32),
            pltpu.VMEM((CY, 128), F32),
            pltpu.VMEM((NQ, NZD, 1, 128), F32),
            pltpu.VMEM((NQ, NZD, 1, 128), F32),
            pltpu.VMEM((NZD, NQ, 1, 128), F32),
            pltpu.VMEM((CX, ROWS, NZ), F32),
            pltpu.VMEM((BATCHES, NQ, 2, 8, 128), F32),
            pltpu.VMEM((BATCHES, NQ, 2, 8, 128), F32),
            pltpu.VMEM((BATCHES, 2, 8, 128), F32),
            pltpu.VMEM((BATCHES, NZD, 8, 128), F32),
            pltpu.VMEM((BATCHES, NQ, 2, 8, 128), F32),
            dma((11,)),
            pltpu.SemaphoreType.REGULAR((2, 3)),
            dma((NQ,)),
            dma((NQ,)),
            dma((NZD,)),
            dma((NZD,)),
            dma((2, 2, CHUNKS)),
            dma((2, 2, CHUNKS)),
            dma((2, 2)),
            dma((2, 2)),
            dma((2, 2, CHUNKS)),
            dma((2, 2, CHUNKS)),
            dma((2, 2)),
            dma((2, 2)),
            dma((BATCHES, NQ)),
            dma((BATCHES, NQ)),
            dma((BATCHES, NZD)),
            dma((BATCHES, NZD)),
            dma((BATCHES, NQ)),
            dma((BATCHES, NQ)),
            dma((2,)),
        ],
        compiler_params=pltpu.CompilerParams(
            collective_id=0, has_side_effects=True, vmem_limit_bytes=24 << 20
        ),
    )(
        *(
            pltpu.with_memory_space_constraint(operand, pltpu.HBM)
            for operand in (
                rollback,
                factors,
                table,
                traces,
                trace_slab.reshape(1, BLOCKS),
                trace_cell,
                trace_shot,
                courant,
                adjoint_prev,
                adjoint_now,
                forward_field,
            )
        )
    )

    return pl.pallas_call(
        update_kernel,
        out_shape=(shape,) * 4,
        in_specs=[smem] + [vmem] * 6,
        out_specs=(anywhere,) * 4,
        scratch_shapes=[pltpu.VMEM((3, CX, CY, NZ), F32), dma((4, CY // UPDATE_ROWS))],
        compiler_params=pltpu.CompilerParams(vmem_limit_bytes=24 << 20),
    )(factors, image, sums, last, courant, first_moment, second_moment)


def solution(mesh):
    in_specs = (
        P("gx", "gy", None),
        P("gx", "gy", None),
        P("gx", "gy", None),
        P("gx", "gy", None),
        P("gx", "gy", None),
        P(None, "gx", "gy", None),
        P("gy", "gx", None),
        P("gy", "gx", None),
        P("gy", "gx"),
        P("gy", "gx"),
        P(),
    )
    out_specs = (P("gx", "gy", None),) * 4
    return jax.shard_map(shards, mesh=mesh, in_specs=in_specs, out_specs=out_specs, check_vma=False)
```
